128 devices in a mesh: fibre: 64 (over y_lo, z, x, core), freq: 2 (over y_hi).
Axes of the slice: x: 4, y: 4 (y_hi: 2, y_lo: 2; y = y_hi * 2 + y_lo), z: 4, core: 2. Of those that a mesh axis runs over, the one named last changes fastest.
Arguments:
- traces: bfloat16 [2, 4096, 4096], P(None, 'fibre'), may hold values from -50 to 50, as said below
- live: int32 [4096], P('fibre'), may hold values 0 or 1
- reach: int32 [64], P('fibre'), may hold values from 1 to 8
Outputs:
- correlations: float32 [64, 8, 64, 64, 128], P('fibre', 'freq')
The draws below stay inside these ranges and needn't reach their ends.
Inputs may be any that keep to these rules, and one draw needn't show every extreme that they name: `traces`: records of the fibre's channels.
All inputs are finite; a program needn't handle non-finite values. No bound on the sum of `live` on one device may be relied on, other than what follows from the above.
Results may differ from the reference program's by a relative error of at most 0.0057.
Values may be sent and summed in bfloat16 or wider, within the bound.
A program may use at most 64 MiB of HBM per device.

```python
import math
import jax
import jax.numpy as jnp
from jax import lax

CH_BLK = 64
NF = 2048
NS = 4096
BAND = 64
OFF = 8
LAGS = 128
WIN = 2
NBLK = 64
CH = 4096


def draw_traces(key, part):
    first_key, gain_key = jax.random.split(key, 2)
    channel_gain = jnp.exp(jax.random.uniform(gain_key, (1, CH, 1), minval=0.0, maxval=math.log(10.0)))
    values = jnp.clip(jax.random.normal(first_key, (WIN, CH, NS)), -5.0, 5.0)
    return jnp.clip(values * channel_gain, -50.0, 50.0).astype(jnp.float32).astype(jnp.bfloat16)


def place_ends(result, key, low, largest):
    shape = result.shape
    place = [jax.random.randint(jax.random.fold_in(key, axis), (), 0, shape[axis]) for axis in range(len(shape))]
    result = result.at[tuple(place)].set(low)
    longest = shape.index(max(shape))
    place[longest] = (place[longest] + 1) % shape[longest]
    return result.at[tuple(place)].set(largest)


def setup_inputs(seed: int = 0) -> dict:
    keys = jax.random.split(jax.random.key(seed), 4)
    traces = draw_traces(jax.random.fold_in(keys[3], 71), 0)
    live = place_ends((jax.random.randint(keys[1], (CH,), 0, 8) < 7).astype(jnp.int32), jax.random.fold_in(keys[1], 1), 0, 1)
    reach = place_ends(jax.random.randint(keys[2], (NBLK,), 1, OFF + 1), jax.random.fold_in(keys[2], 1), 1, OFF).astype(jnp.int32)
    return {"traces": traces, "live": live, "reach": reach}


def phase_angle(freq_ids, sample_ids, period):
    product = freq_ids[:, None] * sample_ids[None, :] % period
    return product.astype(jnp.float32) * (2.0 * math.pi / period)

def reference(traces, live, reach):
    row_count = WIN * CH
    flat_rows = traces.reshape(row_count, NS)
    freq_ids = jnp.arange(NF, dtype=jnp.int32)
    sample_ids = jnp.arange(NS, dtype=jnp.int32)
    angles = phase_angle(freq_ids, sample_ids, NS)
    cosine = jnp.cos(angles).astype(jnp.bfloat16)
    sine_table = (-jnp.sin(angles)).astype(jnp.bfloat16)
    real_part = jnp.dot(flat_rows, cosine.T, preferred_element_type=jnp.float32)
    imag_part = jnp.dot(flat_rows, sine_table.T, preferred_element_type=jnp.float32)
    spectra = jnp.stack([real_part, imag_part])
    band_power = (spectra[0] * spectra[0] + spectra[1] * spectra[1]).reshape(row_count, NF // BAND, BAND).mean(-1)
    whiten_gain = jnp.repeat(1.0 / jnp.sqrt(band_power + 1e-06), BAND, axis=1)
    alive_rows = jnp.tile(live.astype(jnp.float32), WIN)
    whitened = (spectra * whiten_gain[None] * alive_rows[None, :, None]).astype(jnp.bfloat16)
    whitened = whitened.reshape(2, WIN, CH, NF)
    padded = jnp.concatenate([whitened, jnp.zeros((2, WIN, OFF * CH_BLK, NF), jnp.bfloat16)], axis=2)
    lag_steps = jnp.arange(LAGS, dtype=jnp.int32) - LAGS // 2 + NS
    lag_angles = phase_angle(freq_ids, lag_steps, NS)
    lag_table = jnp.concatenate([jnp.cos(lag_angles).astype(jnp.bfloat16), (-jnp.sin(lag_angles)).astype(jnp.bfloat16)])

    def one_block(block_index):
        own_block = lax.dynamic_slice_in_dim(padded, (block_index * CH_BLK).astype(jnp.int32), CH_BLK, 2).astype(jnp.float32)

        def one_offset(offset):
            first = ((block_index + offset) * CH_BLK).astype(jnp.int32)
            partner = lax.dynamic_slice_in_dim(padded, first, CH_BLK, 2).astype(jnp.float32)
            cross_real = (own_block[0][:, :, None, :] * partner[0][:, None, :, :] + own_block[1][:, :, None, :] * partner[1][:, None, :, :]).sum(0)
            cross_imag = (own_block[1][:, :, None, :] * partner[0][:, None, :, :] - own_block[0][:, :, None, :] * partner[1][:, None, :, :]).sum(0)
            cross_block = jnp.stack([cross_real, cross_imag], axis=2).astype(jnp.bfloat16).reshape(CH_BLK * CH_BLK, 2 * NF)
            return jnp.dot(cross_block, lag_table, preferred_element_type=jnp.float32).reshape(CH_BLK, CH_BLK, LAGS)
        return lax.map(one_offset, jnp.arange(OFF, dtype=jnp.int32))
    raw_lags = lax.map(one_block, jnp.arange(NBLK, dtype=jnp.int32))
    keep_mask = (jnp.arange(OFF, dtype=jnp.int32)[None, :] < reach[:, None]).astype(jnp.float32)
    normal_scale = 1.0 / math.sqrt(WIN * NF)
    return raw_lags * normal_scale * keep_mask[:, :, None, None, None]
```

```python
import functools
import math

import jax
import jax.numpy as jnp
import numpy as np
from jax import lax
from jax.experimental import pallas as pl
from jax.experimental.pallas import tpu as pltpu
from jax.sharding import PartitionSpec as P

BAND = 64
OFF = 8
LAGS = 128
F32 = jnp.float32
BF16 = jnp.bfloat16
NT = (((1,), (1,)), ((), ()))


def split_bf16(a):
    hi = a.astype(BF16)
    return hi, (a - hi.astype(F32)).astype(BF16)


def np_split(a):
    import ml_dtypes

    hi = a.astype(np.float32).astype(ml_dtypes.bfloat16)
    lo = (a - hi.astype(np.float64)).astype(np.float32).astype(ml_dtypes.bfloat16)
    return hi, lo


def make_tables():
    l = np.arange(128)
    ang = 2 * np.pi * (np.outer(l, l) % 128) / 128
    fwd = np.concatenate([np.cos(ang), -np.sin(ang)], 1)
    inv = np.concatenate([np.cos(ang), -np.sin(ang)], 0)
    fh, fl = np_split(fwd)
    ih, il = np_split(inv)
    e_fwd = np.concatenate([fh, fl], 0)
    e_inv = np.concatenate([ih, il], 1)
    band = (l[:, None] // BAND == l[None, :] // BAND).astype(np.float32)
    e_band = np.concatenate([band, band], 0).astype(fh.dtype)
    tw = 2 * np.pi * np.outer(np.arange(32), l) / 4096
    twid = np.stack([np.cos(tw), np.sin(tw)]).astype(np.float32)
    return e_fwd, e_inv, e_band, twid


def cadd(a, b):
    return a[0] + b[0], a[1] + b[1]


def csub(a, b):
    return a[0] - b[0], a[1] - b[1]


def cmul_i(a, sign):
    return (-a[1], a[0]) if sign > 0 else (a[1], -a[0])


def crot(a, num, den, sign):
    num %= den
    if num == 0:
        return a
    if 4 * num == den:
        return cmul_i(a, sign)
    if 2 * num == den:
        return -a[0], -a[1]
    if 4 * num == 3 * den:
        return cmul_i(a, -sign)
    if 8 * num % den == 0:
        h = math.sqrt(0.5)
        c = math.copysign(h, math.cos(2 * math.pi * num / den))
        s = sign * math.copysign(h, math.sin(2 * math.pi * num / den))
        if c > 0 and s > 0:
            return (a[0] - a[1]) * h, (a[0] + a[1]) * h
        if c > 0:
            return (a[0] + a[1]) * h, (a[1] - a[0]) * h
        if s > 0:
            return (a[0] + a[1]) * -h, (a[0] - a[1]) * h
        return (a[1] - a[0]) * h, (a[0] + a[1]) * -h
    c = math.cos(2 * math.pi * num / den)
    s = sign * math.sin(2 * math.pi * num / den)
    return a[0] * c - a[1] * s, a[0] * s + a[1] * c


def cfft(xs, sign):
    n = len(xs)
    if n == 1:
        return xs
    half = n // 2
    even = cfft([cadd(xs[i], xs[i + half]) for i in range(half)], sign)
    odd = cfft([crot(csub(xs[i], xs[i + half]), i, n, sign) for i in range(half)], sign)
    out = [None] * n
    out[0::2] = even
    out[1::2] = odd
    return out


def rfft_bins(xs):
    n = len(xs)
    if n == 1:
        return {0: (xs[0], None)}
    half = n // 2
    if xs[half] is None:
        e = d = xs[:half]
    else:
        e = [xs[i] + xs[i + half] for i in range(half)]
        d = [xs[i] - xs[i + half] for i in range(half)]
    out = {2 * k: v for k, v in rfft_bins(e).items()}
    if n == 2:
        out[1] = (d[0], None)
        return out
    q = n // 4
    z = [crot((d[s], -d[s + q]), s, n, -1) for s in range(q)]
    z = cfft(z, -1)
    for v in range(q):
        k = 4 * v + 1
        if k <= half:
            out[k] = z[v]
        else:
            out[n - k] = (z[v][0], -z[v][1])
    return out


def irfft_real(bins, n, keep_half=False):
    if n == 1:
        return [bins[0][0]]
    half = n // 2
    e = irfft_real({k // 2: v for k, v in bins.items() if k % 2 == 0}, half)
    if n == 2:
        d = [bins[1][0]]
    else:
        q = n // 4
        z = []
        for v in range(q):
            k = 4 * v + 1
            if k <= half:
                z.append(bins[k])
            else:
                re, im = bins[n - k]
                z.append((re, -im))
        z = cfft(z, 1)
        y = [crot(z[s], s, n, 1) for s in range(q)]
        d = [v[0] for v in y] + [-v[1] for v in y]
    lower = [e[i] + d[i] for i in range(half)]
    if keep_half:
        return lower
    return lower + [e[i] - d[i] for i in range(half)]


def whiten_to_time(x, live, e_fwd, e_inv, e_band, twid, r, xt, z, spec, pw, yh):
    def tr(q, _):
        col = pl.ds(pl.multiple_of(q * 128, 128), 128)
        for w in range(2):
            part = x[w, :, col].astype(F32)
            xt[col, w * 64 : w * 64 + 64] = part.T
        return 0

    lax.fori_loop(0, 32, tr, 0)

    def dft_l(s, _):
        v = xt[pl.ds(s, 128, stride=32), :].T.astype(BF16)
        g = jnp.dot(jnp.concatenate([v, v], 1), e_fwd[...], preferred_element_type=F32)
        z[0, s] = g[:, :128]
        z[1, s] = g[:, 128:]
        return 0

    lax.fori_loop(0, 32, dft_l, 0)

    def fwd(g, _):
        rows = pl.ds(pl.multiple_of(g * 8, 8), 8)
        for s0 in range(8):
            vals = []
            for s1 in range(4):
                s = 8 * s1 + s0
                a = z[0, s, rows], z[1, s, rows]
                if s:
                    c, n = twid[0, s : s + 1], twid[1, s : s + 1]
                    a = a[0] * c + a[1] * n, a[1] * c - a[0] * n
                vals.append(a)
            vals = cfft(vals, -1)
            for f0 in range(4):
                a = crot(vals[f0], f0 * s0, 32, -1)
                z[0, 8 * f0 + s0, rows], z[1, 8 * f0 + s0, rows] = a
        for f0 in range(4):
            vals = [(z[0, 8 * f0 + s0, rows], z[1, 8 * f0 + s0, rows]) for s0 in range(8)]
            vals = cfft(vals, -1)
            for f1 in range(4):
                f = 4 * f1 + f0
                spec[0, f, rows], spec[1, f, rows] = vals[f1]
                pw[f, rows] = vals[f1][0] * vals[f1][0] + vals[f1][1] * vals[f1][1]
        return 0

    lax.fori_loop(0, 16, fwd, 0)

    alive = jnp.concatenate([live[...], live[...]], 1).astype(F32)
    alive = jnp.broadcast_to(alive, (128, 128)).T * 2.0**-8
    lane = lax.broadcasted_iota(jnp.int32, (128, 128), 1)

    def band_gain(f, _):
        hi, lo = split_bf16(pw[f])
        bp = jnp.dot(jnp.concatenate([hi, lo], 1), e_band[...], preferred_element_type=F32)
        gain = lax.rsqrt(bp * (1.0 / BAND) + 1e-6) * alive
        pw[f] = jnp.where((lane == 0) & (f == 0), gain * math.sqrt(0.5), gain)
        return 0

    lax.fori_loop(0, 16, band_gain, 0)

    def inv(g, _):
        rows = pl.ds(pl.multiple_of(g * 8, 8), 8)
        for f0 in range(4):
            vals = []
            for f1 in range(4):
                f = 4 * f1 + f0
                k = pw[f, rows]
                vals.append((spec[0, f, rows] * k, spec[1, f, rows] * k))
            even = cfft(vals, 1)
            odd = cfft([crot(vals[i], i, 8, 1) for i in range(4)], 1)
            for s0 in range(8):
                a = (even if s0 % 2 == 0 else odd)[s0 // 2]
                a = crot(a, f0 * s0, 32, 1)
                z[0, 8 * f0 + s0, rows], z[1, 8 * f0 + s0, rows] = a
        for s0 in range(8):
            vals = [(z[0, 8 * f0 + s0, rows], z[1, 8 * f0 + s0, rows]) for f0 in range(4)]
            vals = cfft(vals, 1)
            for s1 in range(4):
                s = 8 * s1 + s0
                a = vals[s1]
                if s:
                    c, n = twid[0, s : s + 1], twid[1, s : s + 1]
                    a = a[0] * c - a[1] * n, a[1] * c + a[0] * n
                z[0, s, rows], z[1, s, rows] = a
        return 0

    lax.fori_loop(0, 16, inv, 0)

    def idft_l(s, _):
        both = jnp.concatenate([z[0, s], z[1, s]], 1)
        hi, lo = split_bf16(both)
        d = jnp.dot(jnp.concatenate([hi, lo], 0), e_inv[...], preferred_element_type=F32)
        d = d[:, :128] + d[:, 128:]
        d = (d[:128] + d[128:]).astype(BF16)
        r[s, :, 0:128] = d[:64]
        r[s, :, 128:256] = d[64:]
        return 0

    lax.fori_loop(0, 32, idft_l, 0)


def prepare_own(r, lhs, lhs0):
    def cols(g, _):
        rows = pl.ds(pl.multiple_of(g * 16, 16), 16)
        for h in range(2):
            lanes = slice(128 * h, 128 * h + 128)
            spectra = []
            for n0 in range(2):
                vals = []
                for n1 in range(16):
                    vals.append(r[2 * n1 + n0, rows, lanes].astype(F32))
                vals += [pltpu.roll(v, 127, 1) for v in vals]
                spectra.append(rfft_bins(vals))
            b0, b1 = spectra
            for e, k in enumerate((0, 16)):
                sgn = 1.0 if k == 0 else -1.0
                q0, q1, q2 = b0[k][0], b1[k][0], b0[k][0] * sgn
                for k0, pair in enumerate(((q0, q1), (q1, q2))):
                    for s0 in range(2):
                        at = pl.ds(pl.multiple_of(64 * k0 + g * 16, 16), 16)
                        lhs0[e, at, 256 * s0 + 128 * h : 256 * s0 + 128 * h + 128] = pair[s0].astype(BF16)
            for k in range(1, 16):
                q = [b0[k], b1[k], crot(b0[k], k, 32, 1)]
                q = [(2.0 * a, 2.0 * b) for a, b in q]
                q = [(a.astype(BF16), b.astype(BF16), (-a).astype(BF16)) for a, b in q]
                for k0 in range(2):
                    re_at = pl.ds(pl.multiple_of(64 * k0 + g * 16, 16), 16)
                    im_at = pl.ds(pl.multiple_of(128 + 64 * k0 + g * 16, 16), 16)
                    for s0 in range(2):
                        a, b, na = q[k0 + s0]
                        c0 = 512 * s0 + 128 * h
                        lhs[k - 1, re_at, c0 : c0 + 128] = a
                        lhs[k - 1, re_at, c0 + 256 : c0 + 384] = b
                        lhs[k - 1, im_at, c0 : c0 + 128] = b
                        lhs[k - 1, im_at, c0 + 256 : c0 + 384] = na
        return 0

    lax.fori_loop(0, 4, cols, 0)


def prepare_partner(p, rhs, rhs0):
    def cols(g, _):
        rows = pl.ds(pl.multiple_of(g * 16, 16), 16)
        for h in range(2):
            lanes = slice(128 * h, 128 * h + 128)
            for s0 in range(2):
                vals = [p[2 * s1 + s0, rows, lanes].astype(F32) for s1 in range(16)] + [None] * 16
                bins = rfft_bins(vals)
                for b in range(4):
                    at = pl.ds(pl.multiple_of(64 * b + g * 16, 16), 16)
                    turn = (b - 2) % 128

                    def moved(v):
                        return (pltpu.roll(v, turn, 1) if turn else v).astype(BF16)

                    for e, k in enumerate((0, 16)):
                        rhs0[e, at, 256 * s0 + 128 * h : 256 * s0 + 128 * h + 128] = moved(bins[k][0])
                    for k in range(1, 16):
                        c0 = 512 * s0 + 128 * h
                        rhs[k - 1, at, c0 : c0 + 128] = moved(bins[k][0])
                        rhs[k - 1, at, c0 + 256 : c0 + 384] = moved(bins[k][1])
        return 0

    lax.fori_loop(0, 4, cols, 0)


def multiply(lhs, lhs0, rhs, rhs0, y):
    for e, k in enumerate((0, 16)):
        y[k] = lax.dot_general(lhs0[e], rhs0[e], NT, preferred_element_type=F32).reshape(2, 64, 256)

    def one(k, _):
        d = lax.dot_general(lhs[k], rhs[k], NT, preferred_element_type=F32)
        y[k + 1] = d[:128].reshape(2, 64, 256)
        y[k + 17] = d[128:].reshape(2, 64, 256)
        return 0

    lax.fori_loop(0, 15, one, 0)


def to_lags(y, t, scale):
    def cols(g, _):
        rows = pl.ds(pl.multiple_of(g * 8, 8), 8)
        for k0 in range(2):
            for h in range(2):
                lanes = slice(128 * h, 128 * h + 128)
                bins = {}
                for k in range(17):
                    re = y[k, k0, rows, lanes]
                    im = y[k + 16, k0, rows, lanes] if 0 < k < 16 else None
                    bins[k] = (re, im)
                vals = irfft_real(bins, 32, keep_half=True)
                for k1 in range(16):
                    at = pl.ds(pl.multiple_of(64 * (2 * k1 + k0) + 8 * g, 8), 8)
                    t[h, at, :] = vals[k1] * scale
        return 0

    lax.fori_loop(0, 8, cols, 0)


def place(t, out):
    low = lax.broadcasted_iota(jnp.int32, (32, 128), 1) < 64

    def pair(g, _):
        i0 = 2 * g
        parts = []
        for h in range(2):
            u = t[h, pl.ds(i0, 32, stride=64), :]
            v = t[h, pl.ds(i0 + 1, 32, stride=64), :]
            parts.append(jnp.where(low, u, pltpu.roll(v, 64, 1)))
            parts.append(jnp.where(low, pltpu.roll(u, 64, 1), v))
        m = jnp.concatenate(parts, 0).T
        out[i0] = m[:64]
        out[i0 + 1] = m[64:]
        return 0

    lax.fori_loop(0, 32, pair, 0)


def correlate_all(own, p0, p1, p2, p3, reach, out, lhs, lhs0, rhs, rhs0, y, t, stage, sems):
    first = lax.axis_index("freq") * (OFF // 2)
    prepare_own(own, lhs, lhs0)
    copies = []
    for m, p in enumerate((p0, p1, p2, p3)):
        prepare_partner(p, rhs, rhs0)
        multiply(lhs, lhs0, rhs, rhs0, y)
        keep = jnp.where(first + m < reach[0], 0.5 / 32, 0.0).astype(F32)
        to_lags(y, t, keep)
        if m >= 2:
            copies[m - 2].wait()
        place(t, stage.at[m % 2])
        copies.append(pltpu.make_async_copy(stage.at[m % 2], out.at[m], sems.at[m % 2]))
        copies[m].start()
    copies[2].wait()
    copies[3].wait()


def per_device(blocks, traces, live, reach):
    vmem = pl.BlockSpec(memory_space=pltpu.VMEM)
    params = pltpu.CompilerParams(vmem_limit_bytes=60 * 2**20)
    tables = [jnp.asarray(a) for a in make_tables()]
    r = pl.pallas_call(
        whiten_to_time,
        out_shape=jax.ShapeDtypeStruct((32, 64, 256), BF16),
        in_specs=[vmem] * 6,
        out_specs=vmem,
        scratch_shapes=[
            pltpu.VMEM((4096, 128), F32),
            pltpu.VMEM((2, 32, 128, 128), F32),
            pltpu.VMEM((2, 16, 128, 128), F32),
            pltpu.VMEM((16, 128, 128), F32),
            pltpu.VMEM((8, 128), BF16),
        ],
        compiler_params=params,
    )(traces, live.reshape(1, 64), *tables)
    partners = []
    for m in range(OFF // 2):
        pairs = []
        for b in range(blocks):
            for half in range(2):
                q = b + half * (OFF // 2) + m
                if q < blocks:
                    pairs.append((2 * q + half, 2 * b + half))
        partners.append(lax.ppermute(r, ("fibre", "freq"), pairs))
    out = pl.pallas_call(
        correlate_all,
        out_shape=jax.ShapeDtypeStruct((OFF // 2, 64, 64, LAGS), F32),
        in_specs=[vmem] * 5 + [pl.BlockSpec(memory_space=pltpu.SMEM)],
        out_specs=pl.BlockSpec(memory_space=pl.ANY),
        scratch_shapes=[
            pltpu.VMEM((15, 256, 1024), BF16),
            pltpu.VMEM((2, 128, 512), BF16),
            pltpu.VMEM((15, 256, 1024), BF16),
            pltpu.VMEM((2, 256, 512), BF16),
            pltpu.VMEM((32, 2, 64, 256), F32),
            pltpu.VMEM((2, 2048, 128), F32),
            pltpu.VMEM((2, 64, 64, 128), F32),
            pltpu.SemaphoreType.DMA((2,)),
        ],
        compiler_params=params,
    )(r, *partners, reach)
    return out[None]


def solution(mesh):
    placed = (P(None, "fibre", None), P("fibre"), P("fibre"))
    return jax.shard_map(
        functools.partial(per_device, mesh.shape["fibre"]),
        mesh=mesh,
        in_specs=placed,
        out_specs=P("fibre", "freq", None, None, None),
        check_vma=False,
    )
```

```python
import functools
import math

import jax
import jax.numpy as jnp
import numpy as np
from jax import lax
from jax.experimental import pallas as pl
from jax.experimental.pallas import tpu as pltpu
from jax.sharding import PartitionSpec as P

BAND = 64
OFF = 8
LAGS = 128
F32 = jnp.float32
BF16 = jnp.bfloat16
NT = (((1,), (1,)), ((), ()))


def split_bf16(a):
    hi = a.astype(BF16)
    return hi, (a - hi.astype(F32)).astype(BF16)


def np_split(a):
    import ml_dtypes

    hi = a.astype(np.float32).astype(ml_dtypes.bfloat16)
    lo = (a - hi.astype(np.float64)).astype(np.float32).astype(ml_dtypes.bfloat16)
    return hi, lo


def make_tables():
    l = np.arange(128)
    ang = 2 * np.pi * (np.outer(l, l) % 128) / 128
    fwd = np.concatenate([np.cos(ang), -np.sin(ang)], 1)
    inv = np.concatenate([np.cos(ang), -np.sin(ang)], 0)
    fh, fl = np_split(fwd)
    ih, il = np_split(inv)
    e_fwd = np.concatenate([fh, fl], 0)
    e_inv = np.concatenate([ih, il], 1)
    band = (l[:, None] // BAND == l[None, :] // BAND).astype(np.float32)
    e_band = np.concatenate([band, band], 0).astype(fh.dtype)
    tw = 2 * np.pi * np.outer(np.arange(32), l) / 4096
    twid = np.stack([np.cos(tw), np.sin(tw)]).astype(np.float32)
    return e_fwd, e_inv, e_band, twid


def cadd(a, b):
    return a[0] + b[0], a[1] + b[1]


def csub(a, b):
    return a[0] - b[0], a[1] - b[1]


def cmul_i(a, sign):
    return (-a[1], a[0]) if sign > 0 else (a[1], -a[0])


def crot(a, num, den, sign):
    num %= den
    if num == 0:
        return a
    if 4 * num == den:
        return cmul_i(a, sign)
    if 2 * num == den:
        return -a[0], -a[1]
    if 4 * num == 3 * den:
        return cmul_i(a, -sign)
    if 8 * num % den == 0:
        h = math.sqrt(0.5)
        c = math.copysign(h, math.cos(2 * math.pi * num / den))
        s = sign * math.copysign(h, math.sin(2 * math.pi * num / den))
        if c > 0 and s > 0:
            return (a[0] - a[1]) * h, (a[0] + a[1]) * h
        if c > 0:
            return (a[0] + a[1]) * h, (a[1] - a[0]) * h
        if s > 0:
            return (a[0] + a[1]) * -h, (a[0] - a[1]) * h
        return (a[1] - a[0]) * h, (a[0] + a[1]) * -h
    c = math.cos(2 * math.pi * num / den)
    s = sign * math.sin(2 * math.pi * num / den)
    return a[0] * c - a[1] * s, a[0] * s + a[1] * c


def cfft(xs, sign):
    n = len(xs)
    if n == 1:
        return xs
    half = n // 2
    even = cfft([cadd(xs[i], xs[i + half]) for i in range(half)], sign)
    odd = cfft([crot(csub(xs[i], xs[i + half]), i, n, sign) for i in range(half)], sign)
    out = [None] * n
    out[0::2] = even
    out[1::2] = odd
    return out


def rfft_bins(xs):
    n = len(xs)
    if n == 1:
        return {0: (xs[0], None)}
    half = n // 2
    if xs[half] is None:
        e = d = xs[:half]
    else:
        e = [xs[i] + xs[i + half] for i in range(half)]
        d = [xs[i] - xs[i + half] for i in range(half)]
    out = {2 * k: v for k, v in rfft_bins(e).items()}
    if n == 2:
        out[1] = (d[0], None)
        return out
    q = n // 4
    z = [crot((d[s], -d[s + q]), s, n, -1) for s in range(q)]
    z = cfft(z, -1)
    for v in range(q):
        k = 4 * v + 1
        if k <= half:
            out[k] = z[v]
        else:
            out[n - k] = (z[v][0], -z[v][1])
    return out


def irfft_real(bins, n, keep_half=False):
    if n == 1:
        return [bins[0][0]]
    half = n // 2
    e = irfft_real({k // 2: v for k, v in bins.items() if k % 2 == 0}, half)
    if n == 2:
        d = [bins[1][0]]
    else:
        q = n // 4
        z = []
        for v in range(q):
            k = 4 * v + 1
            if k <= half:
                z.append(bins[k])
            else:
                re, im = bins[n - k]
                z.append((re, -im))
        z = cfft(z, 1)
        y = [crot(z[s], s, n, 1) for s in range(q)]
        d = [v[0] for v in y] + [-v[1] for v in y]
    lower = [e[i] + d[i] for i in range(half)]
    if keep_half:
        return lower
    return lower + [e[i] - d[i] for i in range(half)]


def transpose_in(x, xt):
    def tr(q, _):
        col = pl.ds(pl.multiple_of(q * 128, 128), 128)
        part = jnp.concatenate([x[0, :, col], x[1, :, col]], 0)
        xt[col] = part.T.astype(F32)
        return 0

    lax.fori_loop(0, 32, tr, 0, unroll=8)


def dft_lanes(xt, e_fwd, z):
    def some(q, _):
        v = [xt[pl.ds(8 * q + k, 128, stride=32), :].T.astype(BF16) for k in range(8)]
        v = jnp.concatenate(v, 0)
        g = jnp.dot(jnp.concatenate([v, v], 1), e_fwd[...], preferred_element_type=F32)
        g = g.reshape(8, 128, 256)
        z[0, pl.ds(8 * q, 8)] = g[:, :, :128]
        z[1, pl.ds(8 * q, 8)] = g[:, :, 128:]
        return 0

    lax.fori_loop(0, 4, some, 0)


def fft_steps(z, twid, spec, pw):
    def fwd(g, _):
        rows = pl.ds(pl.multiple_of(g * 8, 8), 8)
        for s0 in range(8):
            vals = []
            for s1 in range(4):
                s = 8 * s1 + s0
                a = z[0, s, rows], z[1, s, rows]
                if s:
                    c, n = twid[0, s : s + 1], twid[1, s : s + 1]
                    a = a[0] * c + a[1] * n, a[1] * c - a[0] * n
                vals.append(a)
            vals = cfft(vals, -1)
            for f0 in range(4):
                a = crot(vals[f0], f0 * s0, 32, -1)
                z[0, 8 * f0 + s0, rows], z[1, 8 * f0 + s0, rows] = a
        for f0 in range(4):
            vals = [(z[0, 8 * f0 + s0, rows], z[1, 8 * f0 + s0, rows]) for s0 in range(8)]
            vals = cfft(vals, -1)
            for f1 in range(4):
                f = 4 * f1 + f0
                spec[0, f, rows], spec[1, f, rows] = vals[f1]
                pw[f, rows] = vals[f1][0] * vals[f1][0] + vals[f1][1] * vals[f1][1]
        return 0

    lax.fori_loop(0, 16, fwd, 0)


def gains(live, e_band, pw):
    alive = jnp.concatenate([live[...], live[...]], 1).astype(F32)
    alive = jnp.broadcast_to(alive, (128, 128)).T * 2.0**-8
    lane = lax.broadcasted_iota(jnp.int32, (128, 128), 1)

    def some(q, _):
        hi, lo = split_bf16(pw[pl.ds(8 * q, 8)].reshape(1024, 128))
        bp = jnp.dot(jnp.concatenate([hi, lo], 1), e_band[...], preferred_element_type=F32)
        bp = bp.reshape(8, 128, 128)
        for k in range(8):
            gain = lax.rsqrt(bp[k] * (1.0 / BAND) + 1e-6) * alive
            if k == 0:
                gain = jnp.where((lane == 0) & (q == 0), gain * math.sqrt(0.5), gain)
            pw[8 * q + k] = gain
        return 0

    lax.fori_loop(0, 2, some, 0)


def ifft_steps(z, twid, spec, pw):
    def inv(g, _):
        rows = pl.ds(pl.multiple_of(g * 8, 8), 8)
        for f0 in range(4):
            vals = []
            for f1 in range(4):
                f = 4 * f1 + f0
                k = pw[f, rows]
                vals.append((spec[0, f, rows] * k, spec[1, f, rows] * k))
            even = cfft(vals, 1)
            odd = cfft([crot(vals[i], i, 8, 1) for i in range(4)], 1)
            for s0 in range(8):
                a = (even if s0 % 2 == 0 else odd)[s0 // 2]
                a = crot(a, f0 * s0, 32, 1)
                z[0, 8 * f0 + s0, rows], z[1, 8 * f0 + s0, rows] = a
        for s0 in range(8):
            vals = [(z[0, 8 * f0 + s0, rows], z[1, 8 * f0 + s0, rows]) for f0 in range(4)]
            vals = cfft(vals, 1)
            for s1 in range(4):
                s = 8 * s1 + s0
                a = vals[s1]
                if s:
                    c, n = twid[0, s : s + 1], twid[1, s : s + 1]
                    a = a[0] * c - a[1] * n, a[1] * c + a[0] * n
                z[0, s, rows], z[1, s, rows] = a
        return 0

    lax.fori_loop(0, 16, inv, 0)


def idft_lanes(z, e_inv, r):
    def some(q, _):
        at = pl.ds(8 * q, 8)
        both = jnp.concatenate([z[0, at].reshape(1024, 128), z[1, at].reshape(1024, 128)], 1)
        hi, lo = split_bf16(both)
        table = e_inv[...]
        d = jnp.dot(hi, table, preferred_element_type=F32)
        d = d + jnp.dot(lo, table, preferred_element_type=F32)
        d = (d[:, :128] + d[:, 128:]).astype(BF16).reshape(8, 2, 64, 128)
        r[at, :, 0:128] = d[:, 0]
        r[at, :, 128:256] = d[:, 1]
        return 0

    lax.fori_loop(0, 4, some, 0)


def whiten_to_time(x, live, e_fwd, e_inv, e_band, twid, r, xt, z, spec, pw):
    transpose_in(x, xt)
    dft_lanes(xt, e_fwd, z)
    fft_steps(z, twid, spec, pw)
    gains(live, e_band, pw)
    ifft_steps(z, twid, spec, pw)
    idft_lanes(z, e_inv, r)


def prepare_own(r, lhs, lhs0):
    def cols(g, _):
        rows = pl.ds(pl.multiple_of(g * 16, 16), 16)
        for h in range(2):
            lanes = slice(128 * h, 128 * h + 128)
            spectra = []
            for n0 in range(2):
                vals = []
                for n1 in range(16):
                    vals.append(r[2 * n1 + n0, rows, lanes].astype(F32))
                vals += [pltpu.roll(v, 127, 1) for v in vals]
                spectra.append(rfft_bins(vals))
            b0, b1 = spectra
            for e, k in enumerate((0, 16)):
                sgn = 1.0 if k == 0 else -1.0
                q0, q1, q2 = b0[k][0], b1[k][0], b0[k][0] * sgn
                for k0, pair in enumerate(((q0, q1), (q1, q2))):
                    for s0 in range(2):
                        at = pl.ds(pl.multiple_of(64 * k0 + g * 16, 16), 16)
                        lhs0[e, at, 256 * s0 + 128 * h : 256 * s0 + 128 * h + 128] = pair[s0].astype(BF16)
            for k in range(1, 16):
                q = [b0[k], b1[k], crot(b0[k], k, 32, 1)]
                q = [(2.0 * a, 2.0 * b) for a, b in q]
                q = [(a.astype(BF16), b.astype(BF16), (-a).astype(BF16)) for a, b in q]
                for k0 in range(2):
                    re_at = pl.ds(pl.multiple_of(64 * k0 + g * 16, 16), 16)
                    im_at = pl.ds(pl.multiple_of(128 + 64 * k0 + g * 16, 16), 16)
                    for s0 in range(2):
                        a, b, na = q[k0 + s0]
                        c0 = 512 * s0 + 128 * h
                        lhs[k - 1, re_at, c0 : c0 + 128] = a
                        lhs[k - 1, re_at, c0 + 256 : c0 + 384] = b
                        lhs[k - 1, im_at, c0 : c0 + 128] = b
                        lhs[k - 1, im_at, c0 + 256 : c0 + 384] = na
        return 0

    lax.fori_loop(0, 4, cols, 0)


def prepare_partner(p, rhs, rhs0):
    def cols(g, _):
        rows = pl.ds(pl.multiple_of(g * 16, 16), 16)
        for h in range(2):
            lanes = slice(128 * h, 128 * h + 128)
            for s0 in range(2):
                vals = [p[2 * s1 + s0, rows, lanes].astype(F32) for s1 in range(16)] + [None] * 16
                bins = rfft_bins(vals)
                for b in range(4):
                    at = pl.ds(pl.multiple_of(64 * b + g * 16, 16), 16)
                    turn = (b - 2) % 128

                    def moved(v):
                        return (pltpu.roll(v, turn, 1) if turn else v).astype(BF16)

                    for e, k in enumerate((0, 16)):
                        rhs0[e, at, 256 * s0 + 128 * h : 256 * s0 + 128 * h + 128] = moved(bins[k][0])
                    for k in range(1, 16):
                        c0 = 512 * s0 + 128 * h
                        rhs[k - 1, at, c0 : c0 + 128] = moved(bins[k][0])
                        rhs[k - 1, at, c0 + 256 : c0 + 384] = moved(bins[k][1])
        return 0

    lax.fori_loop(0, 4, cols, 0)


def multiply(lhs, lhs0, rhs, rhs0, y):
    for e, k in enumerate((0, 16)):
        y[k] = lax.dot_general(lhs0[e], rhs0[e], NT, preferred_element_type=F32).reshape(2, 64, 256)

    def some(q, _):
        for i in range(5):
            k = 5 * q + i
            d = lax.dot_general(lhs[k], rhs[k], NT, preferred_element_type=F32)
            y[k + 1] = d[:128].reshape(2, 64, 256)
            y[k + 17] = d[128:].reshape(2, 64, 256)
        return 0

    lax.fori_loop(0, 3, some, 0)


def to_lags(y, t, scale):
    def cols(g, _):
        rows = pl.ds(pl.multiple_of(g * 8, 8), 8)
        for k0 in range(2):
            for h in range(2):
                lanes = slice(128 * h, 128 * h + 128)
                bins = {}
                for k in range(17):
                    re = y[k, k0, rows, lanes]
                    im = y[k + 16, k0, rows, lanes] if 0 < k < 16 else None
                    bins[k] = (re, im)
                vals = irfft_real(bins, 32, keep_half=True)
                for k1 in range(16):
                    at = pl.ds(pl.multiple_of(64 * (2 * k1 + k0) + 8 * g, 8), 8)
                    t[h, at, :] = vals[k1] * scale
        return 0

    lax.fori_loop(0, 8, cols, 0)


def place(t, out):
    low = lax.broadcasted_iota(jnp.int32, (32, 128), 1) < 64

    def pairs(g, _):
        for n in range(8):
            i0 = 2 * (8 * g + n)
            parts = []
            for h in range(2):
                u = t[h, pl.ds(i0, 32, stride=64), :]
                v = t[h, pl.ds(i0 + 1, 32, stride=64), :]
                parts.append(jnp.where(low, u, pltpu.roll(v, 64, 1)))
                parts.append(jnp.where(low, pltpu.roll(u, 64, 1), v))
            m = jnp.concatenate(parts, 0).T
            out[i0] = m[:64]
            out[i0 + 1] = m[64:]
        return 0

    lax.fori_loop(0, 4, pairs, 0)


MESH = pl.DeviceIdType.MESH


def whole(blocks, x, live, reach, e_fwd, e_inv, e_band, twid, out, xt, z, spec, pw, r, parts, lhs, lhs0, rhs, rhs0, y, t, stage, sent, got, done):
    b = lax.axis_index("fibre")
    half = lax.axis_index("freq")
    first = half * (OFF // 2)

    barrier = pltpu.get_barrier_semaphore()
    greeted = 0
    for m in range(OFF // 2):
        step = first + m
        for other in (b - step, b + step):
            exists = (other >= 0) & (other < blocks) & (step > 0)

            @pl.when(exists)
            def _():
                pl.semaphore_signal(barrier, inc=1, device_id=(other, half), device_id_type=MESH)

            greeted = greeted + jnp.where(exists, 1, 0)

    whiten_to_time(x, live, e_fwd, e_inv, e_band, twid, r, xt, z, spec, pw)
    pl.semaphore_wait(barrier, greeted)

    def copy(m):
        return pltpu.make_async_remote_copy(
            src_ref=r, dst_ref=parts.at[m], send_sem=sent.at[m], recv_sem=got.at[m],
            device_id=(b - first - m, half), device_id_type=MESH,
        )

    for m in range(OFF // 2):

        @pl.when((first + m > 0) & (b - first - m >= 0))
        def _():
            copy(m).start()

    prepare_own(r, lhs, lhs0)
    for m in range(OFF // 2):
        step = first + m

        @pl.when(step == 0)
        def _():
            parts[m] = r[...]

        @pl.when((step > 0) & (b + step >= blocks))
        def _():
            parts[m] = jnp.zeros_like(r)

        @pl.when((step > 0) & (b + step < blocks))
        def _():
            copy(m).wait_recv()

        prepare_partner(parts.at[m], rhs, rhs0)
        multiply(lhs, lhs0, rhs, rhs0, y)
        keep = jnp.where(step < reach[0], 0.5 / 32, 0.0).astype(F32)
        to_lags(y, t, keep)

        def store(n):
            return pltpu.make_async_copy(stage.at[n % 2], out.at[n], done.at[n % 2])

        if m >= 2:
            store(m - 2).wait()
        place(t, stage.at[m % 2])
        store(m).start()
    store(2).wait()
    store(3).wait()
    for m in range(OFF // 2):

        @pl.when((first + m > 0) & (b - first - m >= 0))
        def _():
            copy(m).wait_send()


def per_device(blocks, traces, live, reach):
    vmem = pl.BlockSpec(memory_space=pltpu.VMEM)
    tables = [jnp.asarray(a) for a in make_tables()]
    out = pl.pallas_call(
        functools.partial(whole, blocks),
        out_shape=jax.ShapeDtypeStruct((OFF // 2, 64, 64, LAGS), F32),
        in_specs=[vmem, vmem, pl.BlockSpec(memory_space=pltpu.SMEM)] + [vmem] * 4,
        out_specs=pl.BlockSpec(memory_space=pl.ANY),
        scratch_shapes=[
            pltpu.VMEM((4096, 128), F32),
            pltpu.VMEM((2, 32, 128, 128), F32),
            pltpu.VMEM((2, 16, 128, 128), F32),
            pltpu.VMEM((16, 128, 128), F32),
            pltpu.VMEM((32, 64, 256), BF16),
            pltpu.VMEM((4, 32, 64, 256), BF16),
            pltpu.VMEM((15, 256, 1024), BF16),
            pltpu.VMEM((2, 128, 512), BF16),
            pltpu.VMEM((15, 256, 1024), BF16),
            pltpu.VMEM((2, 256, 512), BF16),
            pltpu.VMEM((32, 2, 64, 256), F32),
            pltpu.VMEM((2, 2048, 128), F32),
            pltpu.VMEM((2, 64, 64, 128), F32),
            pltpu.SemaphoreType.DMA((4,)),
            pltpu.SemaphoreType.DMA((4,)),
            pltpu.SemaphoreType.DMA((2,)),
        ],
        compiler_params=pltpu.CompilerParams(
            vmem_limit_bytes=60 * 2**20, collective_id=0, has_side_effects=True
        ),
    )(traces, live.reshape(1, 64), reach, *tables)
    return out[None]


def solution(mesh):
    placed = (P(None, "fibre", None), P("fibre"), P("fibre"))
    return jax.shard_map(
        functools.partial(per_device, mesh.shape["fibre"]),
        mesh=mesh,
        in_specs=placed,
        out_specs=P("fibre", "freq", None, None, None),
        check_vma=False,
    )
```

```python
import functools
import math

import jax
import jax.numpy as jnp
import numpy as np
from jax import lax
from jax.experimental import pallas as pl
from jax.experimental.pallas import tpu as pltpu
from jax.sharding import PartitionSpec as P

BAND = 64
OFF = 8
LAGS = 128
F32 = jnp.float32
BF16 = jnp.bfloat16
NT = (((1,), (1,)), ((), ()))


def split_bf16(a):
    hi = a.astype(BF16)
    return hi, (a - hi.astype(F32)).astype(BF16)


def np_split(a):
    import ml_dtypes

    hi = a.astype(np.float32).astype(ml_dtypes.bfloat16)
    lo = (a - hi.astype(np.float64)).astype(np.float32).astype(ml_dtypes.bfloat16)
    return hi, lo


def make_tables():
    l = np.arange(128)
    ang = 2 * np.pi * (np.outer(l, l) % 128) / 128
    fwd = np.concatenate([np.cos(ang), -np.sin(ang)], 1)
    inv = np.concatenate([np.cos(ang), -np.sin(ang)], 0)
    fh, fl = np_split(fwd)
    ih, il = np_split(inv)
    e_fwd = np.concatenate([fh, fl], 0)
    e_inv = np.concatenate([ih, il], 1)
    band = (l[:, None] // BAND == l[None, :] // BAND).astype(np.float32)
    e_band = np.concatenate([band, band], 0).astype(fh.dtype)
    tw = 2 * np.pi * np.outer(np.arange(32), l) / 4096
    twid = np.stack([np.cos(tw), np.sin(tw)]).astype(np.float32)
    return e_fwd, e_inv, e_band, twid


def cadd(a, b):
    return a[0] + b[0], a[1] + b[1]


def csub(a, b):
    return a[0] - b[0], a[1] - b[1]


def cmul_i(a, sign):
    return (-a[1], a[0]) if sign > 0 else (a[1], -a[0])


def crot(a, num, den, sign):
    num %= den
    if num == 0:
        return a
    if 4 * num == den:
        return cmul_i(a, sign)
    if 2 * num == den:
        return -a[0], -a[1]
    if 4 * num == 3 * den:
        return cmul_i(a, -sign)
    if 8 * num % den == 0:
        h = math.sqrt(0.5)
        c = math.copysign(h, math.cos(2 * math.pi * num / den))
        s = sign * math.copysign(h, math.sin(2 * math.pi * num / den))
        if c > 0 and s > 0:
            return (a[0] - a[1]) * h, (a[0] + a[1]) * h
        if c > 0:
            return (a[0] + a[1]) * h, (a[1] - a[0]) * h
        if s > 0:
            return (a[0] + a[1]) * -h, (a[0] - a[1]) * h
        return (a[1] - a[0]) * h, (a[0] + a[1]) * -h
    c = math.cos(2 * math.pi * num / den)
    s = sign * math.sin(2 * math.pi * num / den)
    return a[0] * c - a[1] * s, a[0] * s + a[1] * c


def cfft(xs, sign):
    n = len(xs)
    if n == 1:
        return xs
    half = n // 2
    even = cfft([cadd(xs[i], xs[i + half]) for i in range(half)], sign)
    odd = cfft([crot(csub(xs[i], xs[i + half]), i, n, sign) for i in range(half)], sign)
    out = [None] * n
    out[0::2] = even
    out[1::2] = odd
    return out


def rfft_bins(xs):
    n = len(xs)
    if n == 1:
        return {0: (xs[0], None)}
    half = n // 2
    if xs[half] is None:
        e = d = xs[:half]
    else:
        e = [xs[i] + xs[i + half] for i in range(half)]
        d = [xs[i] - xs[i + half] for i in range(half)]
    out = {2 * k: v for k, v in rfft_bins(e).items()}
    if n == 2:
        out[1] = (d[0], None)
        return out
    q = n // 4
    z = [crot((d[s], -d[s + q]), s, n, -1) for s in range(q)]
    z = cfft(z, -1)
    for v in range(q):
        k = 4 * v + 1
        if k <= half:
            out[k] = z[v]
        else:
            out[n - k] = (z[v][0], -z[v][1])
    return out


def irfft_real(bins, n, keep_half=False):
    if n == 1:
        return [bins[0][0]]
    half = n // 2
    e = irfft_real({k // 2: v for k, v in bins.items() if k % 2 == 0}, half)
    if n == 2:
        d = [bins[1][0]]
    else:
        q = n // 4
        z = []
        for v in range(q):
            k = 4 * v + 1
            if k <= half:
                z.append(bins[k])
            else:
                re, im = bins[n - k]
                z.append((re, -im))
        z = cfft(z, 1)
        y = [crot(z[s], s, n, 1) for s in range(q)]
        d = [v[0] for v in y] + [-v[1] for v in y]
    lower = [e[i] + d[i] for i in range(half)]
    if keep_half:
        return lower
    return lower + [e[i] - d[i] for i in range(half)]


def transpose_in(x, xt):
    def tr(q, _):
        col = pl.ds(pl.multiple_of(q * 128, 128), 128)
        part = jnp.concatenate([x[0, :, col], x[1, :, col]], 0)
        xt[col] = part.T.astype(F32)
        return 0

    lax.fori_loop(0, 32, tr, 0, unroll=8)


def dft_lanes(xt, e_fwd, z):
    def some(q, _):
        v = [xt[pl.ds(8 * q + k, 128, stride=32), :].T.astype(BF16) for k in range(8)]
        v = jnp.concatenate(v, 0)
        g = jnp.dot(jnp.concatenate([v, v], 1), e_fwd[...], preferred_element_type=F32)
        g = g.reshape(8, 128, 256)
        z[0, pl.ds(8 * q, 8)] = g[:, :, :128]
        z[1, pl.ds(8 * q, 8)] = g[:, :, 128:]
        return 0

    lax.fori_loop(0, 4, some, 0)


def fft_steps(z, twid, spec, pw):
    def fwd(g, _):
        rows = pl.ds(pl.multiple_of(g * 8, 8), 8)
        for s0 in range(8):
            vals = []
            for s1 in range(4):
                s = 8 * s1 + s0
                a = z[0, s, rows], z[1, s, rows]
                if s:
                    c, n = twid[0, s : s + 1], twid[1, s : s + 1]
                    a = a[0] * c + a[1] * n, a[1] * c - a[0] * n
                vals.append(a)
            vals = cfft(vals, -1)
            for f0 in range(4):
                a = crot(vals[f0], f0 * s0, 32, -1)
                z[0, 8 * f0 + s0, rows], z[1, 8 * f0 + s0, rows] = a
        for f0 in range(4):
            vals = [(z[0, 8 * f0 + s0, rows], z[1, 8 * f0 + s0, rows]) for s0 in range(8)]
            vals = cfft(vals, -1)
            for f1 in range(4):
                f = 4 * f1 + f0
                spec[0, f, rows], spec[1, f, rows] = vals[f1]
                pw[f, rows] = vals[f1][0] * vals[f1][0] + vals[f1][1] * vals[f1][1]
        return 0

    lax.fori_loop(0, 16, fwd, 0)


def gains(live, e_band, pw):
    alive = jnp.concatenate([live[...], live[...]], 1).astype(F32)
    alive = jnp.broadcast_to(alive, (128, 128)).T * 2.0**-8
    lane = lax.broadcasted_iota(jnp.int32, (128, 128), 1)

    def some(q, _):
        hi, lo = split_bf16(pw[pl.ds(8 * q, 8)].reshape(1024, 128))
        bp = jnp.dot(jnp.concatenate([hi, lo], 1), e_band[...], preferred_element_type=F32)
        bp = bp.reshape(8, 128, 128)
        for k in range(8):
            gain = lax.rsqrt(bp[k] * (1.0 / BAND) + 1e-6) * alive
            if k == 0:
                gain = jnp.where((lane == 0) & (q == 0), gain * math.sqrt(0.5), gain)
            pw[8 * q + k] = gain
        return 0

    lax.fori_loop(0, 2, some, 0)


def ifft_steps(z, twid, spec, pw):
    def inv(g, _):
        rows = pl.ds(pl.multiple_of(g * 8, 8), 8)
        for f0 in range(4):
            vals = []
            for f1 in range(4):
                f = 4 * f1 + f0
                k = pw[f, rows]
                vals.append((spec[0, f, rows] * k, spec[1, f, rows] * k))
            even = cfft(vals, 1)
            odd = cfft([crot(vals[i], i, 8, 1) for i in range(4)], 1)
            for s0 in range(8):
                a = (even if s0 % 2 == 0 else odd)[s0 // 2]
                a = crot(a, f0 * s0, 32, 1)
                z[0, 8 * f0 + s0, rows], z[1, 8 * f0 + s0, rows] = a
        for s0 in range(8):
            vals = [(z[0, 8 * f0 + s0, rows], z[1, 8 * f0 + s0, rows]) for f0 in range(4)]
            vals = cfft(vals, 1)
            for s1 in range(4):
                s = 8 * s1 + s0
                a = vals[s1]
                if s:
                    c, n = twid[0, s : s + 1], twid[1, s : s + 1]
                    a = a[0] * c - a[1] * n, a[1] * c + a[0] * n
                z[0, s, rows], z[1, s, rows] = a
        return 0

    lax.fori_loop(0, 16, inv, 0)


def idft_lanes(z, e_inv, r):
    def some(q, _):
        at = pl.ds(8 * q, 8)
        both = jnp.concatenate([z[0, at].reshape(1024, 128), z[1, at].reshape(1024, 128)], 1)
        hi, lo = split_bf16(both)
        table = e_inv[...]
        d = jnp.dot(hi, table, preferred_element_type=F32)
        d = d + jnp.dot(lo, table, preferred_element_type=F32)
        d = (d[:, :128] + d[:, 128:]).astype(BF16).reshape(8, 2, 64, 128)
        r[at, :, 0:128] = d[:, 0]
        r[at, :, 128:256] = d[:, 1]
        return 0

    lax.fori_loop(0, 4, some, 0)


def whiten_to_time(x, live, e_fwd, e_inv, e_band, twid, r, xt, z, spec, pw):
    transpose_in(x, xt)
    dft_lanes(xt, e_fwd, z)
    fft_steps(z, twid, spec, pw)
    gains(live, e_band, pw)
    ifft_steps(z, twid, spec, pw)
    idft_lanes(z, e_inv, r)


def prepare_own(r, lhs, lhs0):
    def cols(g, _):
        rows = pl.ds(pl.multiple_of(g * 16, 16), 16)
        for h in range(2):
            lanes = slice(128 * h, 128 * h + 128)
            spectra = []
            for n0 in range(2):
                vals = []
                for n1 in range(16):
                    vals.append(r[2 * n1 + n0, rows, lanes].astype(F32))
                vals += [pltpu.roll(v, 127, 1) for v in vals]
                spectra.append(rfft_bins(vals))
            b0, b1 = spectra
            for e, k in enumerate((0, 16)):
                sgn = 1.0 if k == 0 else -1.0
                q0, q1, q2 = b0[k][0], b1[k][0], b0[k][0] * sgn
                for k0, pair in enumerate(((q0, q1), (q1, q2))):
                    for s0 in range(2):
                        at = pl.ds(pl.multiple_of(64 * k0 + g * 16, 16), 16)
                        lhs0[e, at, 256 * s0 + 128 * h : 256 * s0 + 128 * h + 128] = pair[s0].astype(BF16)
            for k in range(1, 16):
                q = [b0[k], b1[k], crot(b0[k], k, 32, 1)]
                q = [(2.0 * a, 2.0 * b) for a, b in q]
                q = [(a.astype(BF16), b.astype(BF16), (-a).astype(BF16)) for a, b in q]
                for k0 in range(2):
                    re_at = pl.ds(pl.multiple_of(64 * k0 + g * 16, 16), 16)
                    im_at = pl.ds(pl.multiple_of(128 + 64 * k0 + g * 16, 16), 16)
                    for s0 in range(2):
                        a, b, na = q[k0 + s0]
                        c0 = 512 * s0 + 128 * h
                        lhs[k - 1, re_at, c0 : c0 + 128] = a
                        lhs[k - 1, re_at, c0 + 256 : c0 + 384] = b
                        lhs[k - 1, im_at, c0 : c0 + 128] = b
                        lhs[k - 1, im_at, c0 + 256 : c0 + 384] = na
        return 0

    lax.fori_loop(0, 4, cols, 0)


def prepare_partner(p, rhs, rhs0):
    def cols(g, _):
        rows = pl.ds(pl.multiple_of(g * 16, 16), 16)
        for h in range(2):
            lanes = slice(128 * h, 128 * h + 128)
            for s0 in range(2):
                vals = [p[2 * s1 + s0, rows, lanes].astype(F32) for s1 in range(16)] + [None] * 16
                bins = rfft_bins(vals)
                for b in range(4):
                    at = pl.ds(pl.multiple_of(64 * b + g * 16, 16), 16)
                    turn = (b - 2) % 128

                    def moved(v):
                        return (pltpu.roll(v, turn, 1) if turn else v).astype(BF16)

                    for e, k in enumerate((0, 16)):
                        rhs0[e, at, 256 * s0 + 128 * h : 256 * s0 + 128 * h + 128] = moved(bins[k][0])
                    for k in range(1, 16):
                        c0 = 512 * s0 + 128 * h
                        rhs[k - 1, at, c0 : c0 + 128] = moved(bins[k][0])
                        rhs[k - 1, at, c0 + 256 : c0 + 384] = moved(bins[k][1])
        return 0

    lax.fori_loop(0, 4, cols, 0)


def multiply(lhs, lhs0, rhs, rhs0, y):
    for e, k in enumerate((0, 16)):
        y[k] = lax.dot_general(lhs0[e], rhs0[e], NT, preferred_element_type=F32).reshape(2, 64, 256)

    def some(q, _):
        for i in range(5):
            k = 5 * q + i
            d = lax.dot_general(lhs[k], rhs[k], NT, preferred_element_type=F32)
            y[k + 1] = d[:128].reshape(2, 64, 256)
            y[k + 17] = d[128:].reshape(2, 64, 256)
        return 0

    lax.fori_loop(0, 3, some, 0)


def to_lags(y, t, scale):
    def cols(g, _):
        rows = pl.ds(pl.multiple_of(g * 8, 8), 8)
        for k0 in range(2):
            for h in range(2):
                lanes = slice(128 * h, 128 * h + 128)
                bins = {}
                for k in range(17):
                    re = y[k, k0, rows, lanes]
                    im = y[k + 16, k0, rows, lanes] if 0 < k < 16 else None
                    bins[k] = (re, im)
                vals = irfft_real(bins, 32, keep_half=True)
                for k1 in range(16):
                    at = pl.ds(pl.multiple_of(16 * (2 * k1 + k0) + 8 * (g % 2), 8), 8)
                    t[g // 2, h, at, :] = vals[k1] * scale
        return 0

    lax.fori_loop(0, 8, cols, 0)


def place(t, out):
    low = lax.broadcasted_iota(jnp.int32, (32, 128), 1) < 64
    for i in range(0, 16, 2):
        parts = []
        for h in range(2):
            u = t[0, 0, h, pl.ds(i, 32, stride=16), :]
            v = t[0, 0, h, pl.ds(i + 1, 32, stride=16), :]
            parts.append(jnp.where(low, u, pltpu.roll(v, 64, 1)))
            parts.append(jnp.where(low, pltpu.roll(u, 64, 1), v))
        m = jnp.concatenate(parts, 0).T
        out[0, i] = m[:64]
        out[0, i + 1] = m[64:]


MESH = pl.DeviceIdType.MESH


def whole(chips, x, live, reach, e_fwd, e_inv, e_band, twid, out, xt, z, spec, pw, parts, lhs, lhs0, rhs, rhs0, y, t, sent, got, done):
    fibre = lax.axis_index("fibre")
    half = lax.axis_index("freq")
    c, core = fibre // 2, fibre % 2
    column = c % 4
    near = half == 0
    far = half == 1
    on_a = core == 0
    on_b = core == 1
    own = 4 * half

    def has(k):
        return c + k < chips

    def back(k):
        return c - k >= 0

    barrier = pltpu.get_barrier_semaphore()
    greeted = jnp.int32(0)

    def greet(when, chip, its_core, its_half):
        @pl.when(when)
        def _():
            pl.semaphore_signal(
                barrier, inc=1, device_id=(2 * chip + its_core, its_half), device_id_type=MESH
            )

        return jnp.where(when, 1, 0)

    for k in range(-4, 5):
        within = (c + k >= 0) & (c + k < chips)
        if k:
            greeted = greeted + greet(within, c + k, core, half)
        greeted = greeted + greet(within, c + k, 1 - core, half)
    greeted = greeted + greet(near & on_b & back(3), c - 3, 0, 1)
    greeted = greeted + greet(far & on_a & has(3), c + 3, 1, 0)

    whiten_to_time(x, live, e_fwd, e_inv, e_band, twid, parts.at[own], xt, z, spec, pw)
    pl.semaphore_wait(barrier, greeted)

    def copy(n, src, dst, chip, its_core, its_half):
        return pltpu.make_async_remote_copy(
            src_ref=parts.at[src],
            dst_ref=parts.at[dst],
            send_sem=sent.at[n],
            recv_sem=got.at[n],
            device_id=(2 * chip + its_core, its_half),
            device_id_type=MESH,
        )

    own_a1 = far & on_a & (column == 3) & back(3)
    own_a2 = far & on_a & (column >= 2) & back(2)
    relay_a3 = far & on_b & (column <= 2) & has(4)
    relay_a2 = far & on_b & (column <= 1) & has(4)
    flows = {
        "A1": (near & on_a & back(1), copy(0, 0, 2, c - 1, 0, 0), near & on_a & has(1)),
        "B1": (near & on_b & back(1), copy(1, 0, 2, c - 1, 1, 0), near & on_b & has(1)),
        "A2": (near & on_a & back(2), copy(2, 0, 3, c - 2, 1, 0), near & on_b & has(2)),
        "B0": (near & on_b, copy(3, 0, 1, c, 0, 0), near & on_a),
        "A1s": (near & on_a & has(1), copy(4, 2, 1, c, 1, 0), near & on_b & has(1)),
        "B1s": (near & on_b & has(1), copy(5, 2, 3, c, 0, 0), near & on_a & has(1)),
        "fA4": (far & on_a & back(4), copy(6, 4, 3, c - 4, 1, 1), far & on_b & has(4)),
        "fA3own": (own_a1, copy(7, 4, 1, c - 3, 1, 1), far & on_b & has(3)),
        "fA3": (relay_a3, copy(7, 3, 1, c + 1, 1, 1), None),
        "fA2own": (own_a2, copy(8, 4, 0, c - 2, 0, 1), far & on_a & has(2)),
        "fA2": (relay_a2, copy(8, 3, 0, c + 2, 0, 1), None),
        "fB2": (far & on_b & back(2), copy(9, 4, 1, c - 2, 0, 1), far & on_a & has(2)),
        "fB3": (near & on_b & back(3), copy(10, 0, 3, c - 3, 0, 1), far & on_a & has(3)),
        "fA3s": (far & on_b & has(3), copy(11, 1, 2, c, 0, 1), far & on_a & has(3)),
        "fB2s": (far & on_a & has(2), copy(12, 1, 0, c, 1, 1), far & on_b & has(2)),
        "fB3s": (far & on_a & has(3), copy(13, 3, 2, c, 1, 1), far & on_b & has(3)),
    }

    def send(name):
        @pl.when(flows[name][0])
        def _():
            flows[name][1].start()

    def receive(name):
        @pl.when(flows[name][2])
        def _():
            flows[name][1].wait_recv()

    for name in ("fA4", "fA3own", "fA2own", "fB2", "A1", "B1", "A2", "B0", "fB3"):
        send(name)

    prepare_own(parts.at[own], lhs, lhs0)

    def order(n):
        a0, b0, a1, b1 = ((0, 0, 1, 3), (1, 2, 0, 0), (2, 1, 3, 1), (3, 3, 2, 2))[n]
        return jnp.where(near, jnp.where(on_a, a0, b0), jnp.where(on_a, a1, b1))

    def store(n):
        return pltpu.make_async_copy(t.at[n % 2], out.at[order(n)], done.at[n % 2])

    for n in range(OFF // 2):
        if n == 0:
            receive("fB2"), send("fB2s")
            receive("fA4"), send("fA3"), send("fA2")
        elif n == 1:
            receive("B0")
            receive("B1"), send("B1s")
            receive("fA2own")
            receive("fB2s")
        elif n == 2:
            receive("A1"), send("A1s")
            receive("A1s")
            receive("fB3"), send("fB3s")
            receive("fA3own"), send("fA3s")
        else:
            receive("B1s")
            receive("A2")
            receive("fA3s")
            receive("fB3s")
        m = order(n)
        step = half * (OFF // 2) + m

        @pl.when(fibre + step >= 2 * chips)
        def _():
            parts[m] = jnp.zeros(parts.shape[1:], parts.dtype)

        prepare_partner(parts.at[m], rhs, rhs0)
        multiply(lhs, lhs0, rhs, rhs0, y)
        keep = jnp.where(step < reach[0], 0.5 / 32, 0.0).astype(F32)
        if n >= 2:
            store(n - 2).wait()
        to_lags(y, t.at[n % 2], keep)
        store(n).start()
    store(2).wait()
    store(3).wait()
    for name in flows:

        @pl.when(flows[name][0])
        def _():
            flows[name][1].wait_send()


def per_device(chips, traces, live, reach):
    vmem = pl.BlockSpec(memory_space=pltpu.VMEM)
    tables = [jnp.asarray(a) for a in make_tables()]
    lags = pl.pallas_call(
        functools.partial(whole, chips),
        out_shape=jax.ShapeDtypeStruct((OFF // 2, 4, 2, 512, 128), F32),
        in_specs=[vmem, vmem, pl.BlockSpec(memory_space=pltpu.SMEM)] + [vmem] * 4,
        out_specs=pl.BlockSpec(memory_space=pl.ANY),
        scratch_shapes=[
            pltpu.VMEM((4096, 128), F32),
            pltpu.VMEM((2, 32, 128, 128), F32),
            pltpu.VMEM((2, 16, 128, 128), F32),
            pltpu.VMEM((16, 128, 128), F32),
            pltpu.VMEM((5, 32, 64, 256), BF16),
            pltpu.VMEM((15, 256, 1024), BF16),
            pltpu.VMEM((2, 128, 512), BF16),
            pltpu.VMEM((15, 256, 1024), BF16),
            pltpu.VMEM((2, 256, 512), BF16),
            pltpu.VMEM((32, 2, 64, 256), F32),
            pltpu.VMEM((2, 4, 2, 512, 128), F32),
            pltpu.SemaphoreType.DMA((14,)),
            pltpu.SemaphoreType.DMA((14,)),
            pltpu.SemaphoreType.DMA((2,)),
        ],
        compiler_params=pltpu.CompilerParams(
            vmem_limit_bytes=60 * 2**20, collective_id=0, has_side_effects=True
        ),
    )(traces, live.reshape(1, 64), reach, *tables)
    out = pl.pallas_call(
        place,
        out_shape=jax.ShapeDtypeStruct((OFF // 2, 64, 64, LAGS), F32),
        grid=(OFF // 2, 4),
        in_specs=[pl.BlockSpec((1, 1, 2, 512, 128), lambda m, q: (m, q, 0, 0, 0))],
        out_specs=pl.BlockSpec((1, 16, 64, LAGS), lambda m, q: (m, q, 0, 0)),
    )(lags)
    return out[None]


def solution(mesh):
    placed = (P(None, "fibre", None), P("fibre"), P("fibre"))
    return jax.shard_map(
        functools.partial(per_device, mesh.shape["fibre"] // 2),
        mesh=mesh,
        in_specs=placed,
        out_specs=P("fibre", "freq", None, None, None),
        check_vma=False,
    )
```

```python
import functools
import math

import jax
import jax.numpy as jnp
import numpy as np
from jax import lax
from jax.experimental import pallas as pl
from jax.experimental.pallas import tpu as pltpu
from jax.sharding import PartitionSpec as P

BAND = 64
OFF = 8
LAGS = 128
F32 = jnp.float32
BF16 = jnp.bfloat16
NT = (((1,), (1,)), ((), ()))


def split_bf16(a):
    hi = a.astype(BF16)
    return hi, (a - hi.astype(F32)).astype(BF16)


def np_split(a):
    import ml_dtypes

    hi = a.astype(np.float32).astype(ml_dtypes.bfloat16)
    lo = (a - hi.astype(np.float64)).astype(np.float32).astype(ml_dtypes.bfloat16)
    return hi, lo


def make_tables():
    l = np.arange(128)
    ang = 2 * np.pi * (np.outer(l, l) % 128) / 128
    fwd = np.concatenate([np.cos(ang), -np.sin(ang)], 1)
    inv = np.concatenate([np.cos(ang), -np.sin(ang)], 0)
    fh, fl = np_split(fwd)
    ih, il = np_split(inv)
    e_fwd = np.concatenate([fh, fl], 0)
    e_inv = np.concatenate([ih, il], 1)
    band = (l[:, None] // BAND == l[None, :] // BAND).astype(np.float32)
    e_band = np.concatenate([band, band], 0).astype(fh.dtype)
    tw = 2 * np.pi * np.outer(np.arange(32), l) / 4096
    twid = np.stack([np.cos(tw), np.sin(tw)]).astype(np.float32)
    return e_fwd, e_inv, e_band, twid


def cadd(a, b):
    return a[0] + b[0], a[1] + b[1]


def csub(a, b):
    return a[0] - b[0], a[1] - b[1]


def cmul_i(a, sign):
    return (-a[1], a[0]) if sign > 0 else (a[1], -a[0])


def crot(a, num, den, sign):
    num %= den
    if num == 0:
        return a
    if 4 * num == den:
        return cmul_i(a, sign)
    if 2 * num == den:
        return -a[0], -a[1]
    if 4 * num == 3 * den:
        return cmul_i(a, -sign)
    if 8 * num % den == 0:
        h = math.sqrt(0.5)
        c = math.copysign(h, math.cos(2 * math.pi * num / den))
        s = sign * math.copysign(h, math.sin(2 * math.pi * num / den))
        if c > 0 and s > 0:
            return (a[0] - a[1]) * h, (a[0] + a[1]) * h
        if c > 0:
            return (a[0] + a[1]) * h, (a[1] - a[0]) * h
        if s > 0:
            return (a[0] + a[1]) * -h, (a[0] - a[1]) * h
        return (a[1] - a[0]) * h, (a[0] + a[1]) * -h
    c = math.cos(2 * math.pi * num / den)
    s = sign * math.sin(2 * math.pi * num / den)
    return a[0] * c - a[1] * s, a[0] * s + a[1] * c


def cfft(xs, sign):
    n = len(xs)
    if n == 1:
        return xs
    half = n // 2
    even = cfft([cadd(xs[i], xs[i + half]) for i in range(half)], sign)
    odd = cfft([crot(csub(xs[i], xs[i + half]), i, n, sign) for i in range(half)], sign)
    out = [None] * n
    out[0::2] = even
    out[1::2] = odd
    return out


def rfft_bins(xs):
    n = len(xs)
    if n == 1:
        return {0: (xs[0], None)}
    half = n // 2
    if xs[half] is None:
        e = d = xs[:half]
    else:
        e = [xs[i] + xs[i + half] for i in range(half)]
        d = [xs[i] - xs[i + half] for i in range(half)]
    out = {2 * k: v for k, v in rfft_bins(e).items()}
    if n == 2:
        out[1] = (d[0], None)
        return out
    q = n // 4
    z = [crot((d[s], -d[s + q]), s, n, -1) for s in range(q)]
    z = cfft(z, -1)
    for v in range(q):
        k = 4 * v + 1
        if k <= half:
            out[k] = z[v]
        else:
            out[n - k] = (z[v][0], -z[v][1])
    return out


def irfft_real(bins, n, keep_half=False):
    if n == 1:
        return [bins[0][0]]
    half = n // 2
    e = irfft_real({k // 2: v for k, v in bins.items() if k % 2 == 0}, half)
    if n == 2:
        d = [bins[1][0]]
    else:
        q = n // 4
        z = []
        for v in range(q):
            k = 4 * v + 1
            if k <= half:
                z.append(bins[k])
            else:
                re, im = bins[n - k]
                z.append((re, -im))
        z = cfft(z, 1)
        y = [crot(z[s], s, n, 1) for s in range(q)]
        d = [v[0] for v in y] + [-v[1] for v in y]
    lower = [e[i] + d[i] for i in range(half)]
    if keep_half:
        return lower
    return lower + [e[i] - d[i] for i in range(half)]


def transpose_in(x, xt):
    def tr(q, _):
        col = pl.ds(pl.multiple_of(q * 128, 128), 128)
        part = jnp.concatenate([x[0, :, col], x[1, :, col]], 0)
        xt[col] = part.T.astype(F32)
        return 0

    lax.fori_loop(0, 32, tr, 0, unroll=8)


def dft_lanes(xt, e_fwd, z):
    def some(q, _):
        v = [xt[pl.ds(8 * q + k, 128, stride=32), :].T.astype(BF16) for k in range(8)]
        v = jnp.concatenate(v, 0)
        g = jnp.dot(jnp.concatenate([v, v], 1), e_fwd[...], preferred_element_type=F32)
        g = g.reshape(8, 128, 256)
        z[0, pl.ds(8 * q, 8)] = g[:, :, :128]
        z[1, pl.ds(8 * q, 8)] = g[:, :, 128:]
        return 0

    lax.fori_loop(0, 4, some, 0)


def fft_steps(z, twid, spec, pw):
    def fwd(g, _):
        rows = pl.ds(pl.multiple_of(g * 8, 8), 8)
        for s0 in range(8):
            vals = []
            for s1 in range(4):
                s = 8 * s1 + s0
                a = z[0, s, rows], z[1, s, rows]
                if s:
                    c, n = twid[0, s : s + 1], twid[1, s : s + 1]
                    a = a[0] * c + a[1] * n, a[1] * c - a[0] * n
                vals.append(a)
            vals = cfft(vals, -1)
            for f0 in range(4):
                a = crot(vals[f0], f0 * s0, 32, -1)
                z[0, 8 * f0 + s0, rows], z[1, 8 * f0 + s0, rows] = a
        for f0 in range(4):
            vals = [(z[0, 8 * f0 + s0, rows], z[1, 8 * f0 + s0, rows]) for s0 in range(8)]
            vals = cfft(vals, -1)
            for f1 in range(4):
                f = 4 * f1 + f0
                spec[0, f, rows], spec[1, f, rows] = vals[f1]
                pw[f, rows] = vals[f1][0] * vals[f1][0] + vals[f1][1] * vals[f1][1]
        return 0

    lax.fori_loop(0, 16, fwd, 0)


def gains(live, e_band, pw):
    alive = jnp.concatenate([live[...], live[...]], 1).astype(F32)
    alive = jnp.broadcast_to(alive, (128, 128)).T * 2.0**-8
    lane = lax.broadcasted_iota(jnp.int32, (128, 128), 1)

    def some(q, _):
        hi, lo = split_bf16(pw[pl.ds(8 * q, 8)].reshape(1024, 128))
        bp = jnp.dot(jnp.concatenate([hi, lo], 1), e_band[...], preferred_element_type=F32)
        bp = bp.reshape(8, 128, 128)
        for k in range(8):
            gain = lax.rsqrt(bp[k] * (1.0 / BAND) + 1e-6) * alive
            if k == 0:
                gain = jnp.where((lane == 0) & (q == 0), gain * math.sqrt(0.5), gain)
            pw[8 * q + k] = gain
        return 0

    lax.fori_loop(0, 2, some, 0)


def ifft_steps(z, twid, spec, pw):
    def inv(g, _):
        rows = pl.ds(pl.multiple_of(g * 8, 8), 8)
        for f0 in range(4):
            vals = []
            for f1 in range(4):
                f = 4 * f1 + f0
                k = pw[f, rows]
                vals.append((spec[0, f, rows] * k, spec[1, f, rows] * k))
            even = cfft(vals, 1)
            odd = cfft([crot(vals[i], i, 8, 1) for i in range(4)], 1)
            for s0 in range(8):
                a = (even if s0 % 2 == 0 else odd)[s0 // 2]
                a = crot(a, f0 * s0, 32, 1)
                z[0, 8 * f0 + s0, rows], z[1, 8 * f0 + s0, rows] = a
        for s0 in range(8):
            vals = [(z[0, 8 * f0 + s0, rows], z[1, 8 * f0 + s0, rows]) for f0 in range(4)]
            vals = cfft(vals, 1)
            for s1 in range(4):
                s = 8 * s1 + s0
                a = vals[s1]
                if s:
                    c, n = twid[0, s : s + 1], twid[1, s : s + 1]
                    a = a[0] * c - a[1] * n, a[1] * c + a[0] * n
                z[0, s, rows], z[1, s, rows] = a
        return 0

    lax.fori_loop(0, 16, inv, 0)


def idft_lanes(z, e_inv, r):
    def some(q, _):
        at = pl.ds(8 * q, 8)
        both = jnp.concatenate([z[0, at].reshape(1024, 128), z[1, at].reshape(1024, 128)], 1)
        hi, lo = split_bf16(both)
        table = e_inv[...]
        d = jnp.dot(hi, table, preferred_element_type=F32)
        d = d + jnp.dot(lo, table, preferred_element_type=F32)
        d = (d[:, :128] + d[:, 128:]).astype(BF16).reshape(8, 2, 64, 128)
        r[at, :, 0:128] = d[:, 0]
        r[at, :, 128:256] = d[:, 1]
        return 0

    lax.fori_loop(0, 4, some, 0)


def whiten_begin(x, e_fwd, xt, z):
    transpose_in(x, xt)
    dft_lanes(xt, e_fwd, z)


def whiten_end(live, e_inv, e_band, twid, r, z, spec, pw):
    fft_steps(z, twid, spec, pw)
    gains(live, e_band, pw)
    ifft_steps(z, twid, spec, pw)
    idft_lanes(z, e_inv, r)


def prepare_own(r, lhs, lhs0):
    def cols(g, _):
        rows = pl.ds(pl.multiple_of(g * 16, 16), 16)
        for h in range(2):
            lanes = slice(128 * h, 128 * h + 128)
            spectra = []
            for n0 in range(2):
                vals = [r[2 * n1 + n0, rows, lanes].astype(F32) for n1 in range(16)]
                vals += [pltpu.roll(v, 127, 1) for v in vals]
                spectra.append(rfft_bins(vals))
            b0, b1 = spectra
            for e, k in enumerate((0, 16)):
                last = b0[k][0] if k == 0 else -b0[k][0]
                for n0, v in enumerate((b0[k][0], b1[k][0], last)):
                    lhs0[e, n0, rows, lanes] = v.astype(BF16)
            for k in range(1, 16):
                for n0, v in enumerate((b0[k], b1[k], crot(b0[k], k, 32, 1))):
                    re, im = (2.0 * v[0]).astype(BF16), (2.0 * v[1]).astype(BF16)
                    lhs[k - 1, 3 * n0, rows, lanes] = re
                    lhs[k - 1, 3 * n0 + 1, rows, lanes] = im
                    lhs[k - 1, 3 * n0 + 2, rows, lanes] = -re
        return 0

    lax.fori_loop(0, 4, cols, 0)


def prepare_partner(p, rhs, rhs0):
    def cols(g, _):
        rows = pl.ds(pl.multiple_of(g * 16, 16), 16)
        for h in range(2):
            lanes = slice(128 * h, 128 * h + 128)
            for s0 in range(2):
                vals = [p[2 * s1 + s0, rows, lanes].astype(F32) for s1 in range(16)] + [None] * 16
                bins = rfft_bins(vals)
                c0 = 256 * s0 + 128 * h
                for e, k in enumerate((0, 16)):
                    rhs0[e, rows, c0 : c0 + 128] = bins[k][0].astype(BF16)
                c0 = 512 * s0 + 128 * h
                for k in range(1, 16):
                    rhs[k - 1, rows, c0 : c0 + 128] = bins[k][0].astype(BF16)
                    rhs[k - 1, rows, c0 + 256 : c0 + 384] = bins[k][1].astype(BF16)
        return 0

    lax.fori_loop(0, 4, cols, 0)


def turned(v):
    tiles = [v[:, i : i + 128] for i in range(0, v.shape[1], 128)]
    rows = []
    for b in range(4):
        rows.append(v if b == 2 else jnp.concatenate([pltpu.roll(a, (b - 2) % 128, 1) for a in tiles], 1))
    return jnp.concatenate(rows, 0)


def multiply(lhs, lhs0, rhs, rhs0, y):
    def product(quads, partner):
        a = jnp.concatenate([jnp.concatenate(q, 1) for q in quads], 0)
        return lax.dot_general(a, turned(partner), NT, preferred_element_type=F32)

    for e, k in enumerate((0, 16)):
        a = [lhs0[e, n0] for n0 in range(3)]
        y[k] = product((a[:2], a[1:]), rhs0[e]).reshape(2, 64, 256)
    for k in range(15):
        re, im, neg = ([lhs[k, 3 * n0 + c] for n0 in range(3)] for c in range(3))
        quads = [(re[n], im[n], re[n + 1], im[n + 1]) for n in range(2)]
        quads += [(im[n], neg[n], im[n + 1], neg[n + 1]) for n in range(2)]
        d = product(quads, rhs[k])
        y[k + 1] = d[:128].reshape(2, 64, 256)
        y[k + 17] = d[128:].reshape(2, 64, 256)


def to_lags(y, t, scale):
    def cols(g, _):
        rows = pl.ds(pl.multiple_of(g * 8, 8), 8)
        for k0 in range(2):
            for h in range(2):
                lanes = slice(128 * h, 128 * h + 128)
                bins = {}
                for k in range(17):
                    re = y[k, k0, rows, lanes]
                    im = y[k + 16, k0, rows, lanes] if 0 < k < 16 else None
                    bins[k] = (re, im)
                vals = irfft_real(bins, 32, keep_half=True)
                for k1 in range(16):
                    at = pl.ds(pl.multiple_of(16 * (2 * k1 + k0) + 8 * (g % 2), 8), 8)
                    t[g // 2, h, at, :] = vals[k1] * scale
        return 0

    lax.fori_loop(0, 8, cols, 0)


def place(t, out):
    low = lax.broadcasted_iota(jnp.int32, (32, 128), 1) < 64
    for q in range(4):
        for i in range(0, 16, 2):
            parts = []
            for h in range(2):
                u = t[0, q, h, pl.ds(i, 32, stride=16), :]
                v = t[0, q, h, pl.ds(i + 1, 32, stride=16), :]
                parts.append(jnp.where(low, u, pltpu.roll(v, 64, 1)))
                parts.append(jnp.where(low, pltpu.roll(u, 64, 1), v))
            m = jnp.concatenate(parts, 0).T
            out[0, 16 * q + i] = m[:64]
            out[0, 16 * q + i + 1] = m[64:]


MESH = pl.DeviceIdType.MESH


def whole(chips, x, live, reach, e_fwd, e_inv, e_band, twid, out, xt, z, spec, pw, x_far, live_far, parts, lhs, lhs0, rhs, rhs0, y, t, sent, got, done):
    fibre = lax.axis_index("fibre")
    half = lax.axis_index("freq")
    c, core = fibre // 2, fibre % 2
    column = c % 4
    near = half == 0
    far = half == 1
    on_a = core == 0
    on_b = core == 1
    own = 4 * half

    def has(k):
        return c + k < chips

    def back(k):
        return c - k >= 0

    barrier = pltpu.get_barrier_semaphore()
    greeted = jnp.int32(0)

    def greet(when, chip, its_core, its_half):
        @pl.when(when)
        def _():
            pl.semaphore_signal(
                barrier, inc=1, device_id=(2 * chip + its_core, its_half), device_id_type=MESH
            )

        return jnp.where(when, 1, 0)

    for k in range(-4, 5):
        within = (c + k >= 0) & (c + k < chips)
        if k:
            greeted = greeted + greet(within, c + k, core, half)
        greeted = greeted + greet(within, c + k, 1 - core, half)
    greeted = greeted + greet(near & on_b & back(3), c - 3, 0, 1)
    greeted = greeted + greet(far & on_a & has(3), c + 3, 1, 0)

    whiten_begin(x, e_fwd, xt, z)
    pl.semaphore_wait(barrier, greeted)

    def copy(n, src, dst, chip, its_core, its_half):
        return pltpu.make_async_remote_copy(
            src_ref=parts.at[src] if isinstance(src, (int, jax.Array)) else src,
            dst_ref=parts.at[dst] if isinstance(dst, (int, jax.Array)) else dst,
            send_sem=sent.at[n],
            recv_sem=got.at[n],
            device_id=(2 * chip + its_core, its_half),
            device_id_type=MESH,
        )

    own_a1 = far & on_a & (column == 3) & back(3)
    own_a2 = far & on_a & (column >= 2) & back(2)
    relay_a3 = far & on_b & (column <= 2) & has(4)
    relay_a2 = far & on_b & (column <= 1) & has(4)
    flows = {
        "A1": (near & on_a & back(1), copy(0, 0, 1, c - 1, 1, 0), near & on_b & has(1)),
        "B1": (near & on_b & back(1), copy(1, 0, 2, c - 1, 1, 0), near & on_b & has(1)),
        "A2": (near & on_a & back(2), copy(2, 0, 3, c - 2, 1, 0), near & on_b & has(2)),
        "B0": (near & on_b, copy(3, 0, 1, c, 0, 0), near & on_a),
        "A1s": (near & on_b & has(1), copy(4, 1, 2, c, 0, 0), near & on_a & has(1)),
        "B1s": (near & on_b & has(1), copy(5, 2, 3, c, 0, 0), near & on_a & has(1)),
        "fX4": (far & on_a & back(4), copy(6, x, x_far, c - 4, 1, 1), far & on_b & has(4)),
        "fL4": (far & on_a & back(4), copy(14, live, live_far, c - 4, 1, 1), far & on_b & has(4)),
        "fA3own": (own_a1, copy(7, 4, 1, c - 3, 1, 1), far & on_b & has(3)),
        "fA3": (relay_a3, copy(7, 3, 1, c + 1, 1, 1), None),
        "fA2own": (own_a2, copy(8, 4, 0, c - 2, 0, 1), far & on_a & has(2)),
        "fA2": (relay_a2, copy(8, 3, 0, c + 2, 0, 1), None),
        "fB2": (far & on_b & back(2), copy(9, 4, 1, c - 2, 0, 1), far & on_a & has(2)),
        "fB3": (near & on_b & back(3), copy(10, 0, 3, c - 3, 0, 1), far & on_a & has(3)),
        "fA3s": (far & on_b & has(3), copy(11, 1, 2, c, 0, 1), far & on_a & has(3)),
        "fB2s": (far & on_a & has(2), copy(12, 1, 0, c, 1, 1), far & on_b & has(2)),
        "fB3s": (far & on_a & has(3), copy(13, 3, 2, c, 1, 1), far & on_b & has(3)),
    }

    def send_if(name, when):
        @pl.when(flows[name][0] & when)
        def _():
            flows[name][1].start()

    def receive_if(name, when):
        @pl.when(flows[name][2] & when)
        def _():
            flows[name][1].wait_recv()

    def send(name):
        send_if(name, True)

    def receive(name):
        receive_if(name, True)

    send("fX4"), send("fL4")
    whiten_end(live, e_inv, e_band, twid, parts.at[own], z, spec, pw)
    for name in ("fA3own", "fA2own", "fB2", "fB3", "A1", "B0"):
        send(name)

    prepare_own(parts.at[own], lhs, lhs0)

    receive("fX4"), receive("fL4")

    @pl.when(far & on_b & has(4))
    def _():
        whiten_begin(x_far, e_fwd, xt, z)
        whiten_end(live_far, e_inv, e_band, twid, parts.at[3], z, spec, pw)

    send("fA2"), send("fA3")

    def order(n):
        a0, b0, a1, b1 = ((0, 0, 1, 3), (1, 1, 0, 0), (2, 2, 3, 1), (3, 3, 2, 2))[n]
        if n in (1, 2):
            a1 = jnp.where(column >= 2, (0, 3, 0)[n], a1)
        return jnp.where(near, jnp.where(on_a, a0, b0), jnp.where(on_a, a1, b1))

    def store(n):
        return pltpu.make_async_copy(t.at[n % 2], out.at[order(n)], done.at[n % 2])

    for n in range(OFF // 2):
        if n == 0:
            receive("fB2"), send("fB2s")
        elif n == 1:
            send("B1"), send("A2")
            receive("B0")
            receive("A1"), send("A1s")
            receive_if("fA2own", column < 2)
            receive_if("fB3", column >= 2), send_if("fB3s", column >= 2)
            receive("fB2s")
        elif n == 2:
            receive("B1"), send("B1s")
            receive("A1s")
            receive_if("fB3", column < 2), send_if("fB3s", column < 2)
            receive_if("fA2own", column >= 2)
            receive("fA3own"), send("fA3s")
        else:
            receive("B1s")
            receive("A2")
            receive("fA3s")
            receive("fB3s")
        m = order(n)
        step = half * (OFF // 2) + m

        @pl.when(fibre + step >= 2 * chips)
        def _():
            parts[m] = jnp.zeros(parts.shape[1:], parts.dtype)

        prepare_partner(parts.at[m], rhs, rhs0)
        multiply(lhs, lhs0, rhs, rhs0, y)
        keep = jnp.where(step < reach[0], 0.5 / 32, 0.0).astype(F32)
        if n >= 2:
            store(n - 2).wait()
        to_lags(y, t.at[n % 2], keep)
        store(n).start()
    store(2).wait()
    store(3).wait()
    for name in flows:

        @pl.when(flows[name][0])
        def _():
            flows[name][1].wait_send()


def per_device(chips, traces, live, reach):
    vmem = pl.BlockSpec(memory_space=pltpu.VMEM)
    tables = [jnp.asarray(a) for a in make_tables()]
    lags = pl.pallas_call(
        functools.partial(whole, chips),
        out_shape=jax.ShapeDtypeStruct((OFF // 2, 4, 2, 512, 128), F32),
        in_specs=[vmem, vmem, pl.BlockSpec(memory_space=pltpu.SMEM)] + [vmem] * 4,
        out_specs=pl.BlockSpec(memory_space=pl.ANY),
        scratch_shapes=[
            pltpu.VMEM((4096, 128), F32),
            pltpu.VMEM((2, 32, 128, 128), F32),
            pltpu.VMEM((2, 16, 128, 128), F32),
            pltpu.VMEM((16, 128, 128), F32),
            pltpu.VMEM((2, 64, 4096), BF16),
            pltpu.VMEM((1, 64), jnp.int32),
            pltpu.VMEM((5, 32, 64, 256), BF16),
            pltpu.VMEM((15, 9, 64, 256), BF16),
            pltpu.VMEM((2, 3, 64, 256), BF16),
            pltpu.VMEM((15, 64, 1024), BF16),
            pltpu.VMEM((2, 64, 512), BF16),
            pltpu.VMEM((32, 2, 64, 256), F32),
            pltpu.VMEM((2, 4, 2, 512, 128), F32),
            pltpu.SemaphoreType.DMA((15,)),
            pltpu.SemaphoreType.DMA((15,)),
            pltpu.SemaphoreType.DMA((2,)),
        ],
        compiler_params=pltpu.CompilerParams(
            vmem_limit_bytes=60 * 2**20, collective_id=0, has_side_effects=True
        ),
    )(traces, live.reshape(1, 64), reach, *tables)
    out = pl.pallas_call(
        place,
        out_shape=jax.ShapeDtypeStruct((OFF // 2, 64, 64, LAGS), F32),
        grid=(OFF // 2,),
        in_specs=[pl.BlockSpec((1, 4, 2, 512, 128), lambda m: (m, 0, 0, 0, 0))],
        out_specs=pl.BlockSpec((1, 64, 64, LAGS), lambda m: (m, 0, 0, 0)),
    )(lags)
    return out[None]


def solution(mesh):
    placed = (P(None, "fibre", None), P("fibre"), P("fibre"))
    return jax.shard_map(
        functools.partial(per_device, mesh.shape["fibre"] // 2),
        mesh=mesh,
        in_specs=placed,
        out_specs=P("fibre", "freq", None, None, None),
        check_vma=False,
    )
```

```python
import functools
import math

import jax
import jax.numpy as jnp
import numpy as np
from jax import lax
from jax.experimental import pallas as pl
from jax.experimental.pallas import tpu as pltpu
from jax.sharding import PartitionSpec as P

BAND = 64
OFF = 8
LAGS = 128
F32 = jnp.float32
BF16 = jnp.bfloat16
NT = (((1,), (1,)), ((), ()))


def split_bf16(a):
    hi = a.astype(BF16)
    return hi, (a - hi.astype(F32)).astype(BF16)


def np_split(a):
    import ml_dtypes

    hi = a.astype(np.float32).astype(ml_dtypes.bfloat16)
    lo = (a - hi.astype(np.float64)).astype(np.float32).astype(ml_dtypes.bfloat16)
    return hi, lo


def make_tables():
    l = np.arange(128)
    ang = 2 * np.pi * (np.outer(l, l) % 128) / 128
    fwd = np.concatenate([np.cos(ang), -np.sin(ang)], 1)
    inv = np.concatenate([np.cos(ang), -np.sin(ang)], 0)
    fh, fl = np_split(fwd)
    ih, il = np_split(inv)
    e_fwd = np.concatenate([fh, fl], 0)
    e_inv = np.concatenate([ih, il], 1)
    band = (l[:, None] // BAND == l[None, :] // BAND).astype(np.float32)
    e_band = np.concatenate([band, band], 0).astype(fh.dtype)
    tw = 2 * np.pi * np.outer(np.arange(32), l) / 4096
    twid = np.stack([np.cos(tw), np.sin(tw)]).astype(np.float32)
    return e_fwd, e_inv, e_band, twid


def cadd(a, b):
    return a[0] + b[0], a[1] + b[1]


def csub(a, b):
    return a[0] - b[0], a[1] - b[1]


def cmul_i(a, sign):
    return (-a[1], a[0]) if sign > 0 else (a[1], -a[0])


def crot(a, num, den, sign):
    num %= den
    if num == 0:
        return a
    if 4 * num == den:
        return cmul_i(a, sign)
    if 2 * num == den:
        return -a[0], -a[1]
    if 4 * num == 3 * den:
        return cmul_i(a, -sign)
    if 8 * num % den == 0:
        h = math.sqrt(0.5)
        c = math.copysign(h, math.cos(2 * math.pi * num / den))
        s = sign * math.copysign(h, math.sin(2 * math.pi * num / den))
        if c > 0 and s > 0:
            return (a[0] - a[1]) * h, (a[0] + a[1]) * h
        if c > 0:
            return (a[0] + a[1]) * h, (a[1] - a[0]) * h
        if s > 0:
            return (a[0] + a[1]) * -h, (a[0] - a[1]) * h
        return (a[1] - a[0]) * h, (a[0] + a[1]) * -h
    c = math.cos(2 * math.pi * num / den)
    s = sign * math.sin(2 * math.pi * num / den)
    return a[0] * c - a[1] * s, a[0] * s + a[1] * c


def cfft(xs, sign):
    n = len(xs)
    if n == 1:
        return xs
    half = n // 2
    even = cfft([cadd(xs[i], xs[i + half]) for i in range(half)], sign)
    odd = cfft([crot(csub(xs[i], xs[i + half]), i, n, sign) for i in range(half)], sign)
    out = [None] * n
    out[0::2] = even
    out[1::2] = odd
    return out


def rfft_bins(xs):
    n = len(xs)
    if n == 1:
        return {0: (xs[0], None)}
    half = n // 2
    if xs[half] is None:
        e = d = xs[:half]
    else:
        e = [xs[i] + xs[i + half] for i in range(half)]
        d = [xs[i] - xs[i + half] for i in range(half)]
    out = {2 * k: v for k, v in rfft_bins(e).items()}
    if n == 2:
        out[1] = (d[0], None)
        return out
    q = n // 4
    z = [crot((d[s], -d[s + q]), s, n, -1) for s in range(q)]
    z = cfft(z, -1)
    for v in range(q):
        k = 4 * v + 1
        if k <= half:
            out[k] = z[v]
        else:
            out[n - k] = (z[v][0], -z[v][1])
    return out


def irfft_real(bins, n, keep_half=False):
    if n == 1:
        return [bins[0][0]]
    half = n // 2
    e = irfft_real({k // 2: v for k, v in bins.items() if k % 2 == 0}, half)
    if n == 2:
        d = [bins[1][0]]
    else:
        q = n // 4
        z = []
        for v in range(q):
            k = 4 * v + 1
            if k <= half:
                z.append(bins[k])
            else:
                re, im = bins[n - k]
                z.append((re, -im))
        z = cfft(z, 1)
        y = [crot(z[s], s, n, 1) for s in range(q)]
        d = [v[0] for v in y] + [-v[1] for v in y]
    lower = [e[i] + d[i] for i in range(half)]
    if keep_half:
        return lower
    return lower + [e[i] - d[i] for i in range(half)]


def transpose_in(x, xt):
    def tr(q, _):
        col = pl.ds(pl.multiple_of(q * 128, 128), 128)
        part = jnp.concatenate([x[0, :, col], x[1, :, col]], 0)
        xt[col] = part.T.astype(F32)
        return 0

    lax.fori_loop(0, 32, tr, 0, unroll=8)


def dft_lanes(xt, e_fwd, z):
    def some(q, _):
        v = [xt[pl.ds(8 * q + k, 128, stride=32), :].T.astype(BF16) for k in range(8)]
        v = jnp.concatenate(v, 0)
        g = jnp.dot(jnp.concatenate([v, v], 1), e_fwd[...], preferred_element_type=F32)
        g = g.reshape(8, 128, 256)
        z[0, pl.ds(8 * q, 8)] = g[:, :, :128]
        z[1, pl.ds(8 * q, 8)] = g[:, :, 128:]
        return 0

    lax.fori_loop(0, 4, some, 0)


def fft_steps(z, twid, spec, pw):
    def fwd(g, _):
        rows = pl.ds(pl.multiple_of(g * 8, 8), 8)
        for s0 in range(8):
            vals = []
            for s1 in range(4):
                s = 8 * s1 + s0
                a = z[0, s, rows], z[1, s, rows]
                if s:
                    c, n = twid[0, s : s + 1], twid[1, s : s + 1]
                    a = a[0] * c + a[1] * n, a[1] * c - a[0] * n
                vals.append(a)
            vals = cfft(vals, -1)
            for f0 in range(4):
                a = crot(vals[f0], f0 * s0, 32, -1)
                z[0, 8 * f0 + s0, rows], z[1, 8 * f0 + s0, rows] = a
        for f0 in range(4):
            vals = [(z[0, 8 * f0 + s0, rows], z[1, 8 * f0 + s0, rows]) for s0 in range(8)]
            vals = cfft(vals, -1)
            for f1 in range(4):
                f = 4 * f1 + f0
                spec[0, f, rows], spec[1, f, rows] = vals[f1]
                pw[f, rows] = vals[f1][0] * vals[f1][0] + vals[f1][1] * vals[f1][1]
        return 0

    lax.fori_loop(0, 16, fwd, 0)


def gains(live, e_band, pw):
    alive = jnp.concatenate([live[...], live[...]], 1).astype(F32)
    alive = jnp.broadcast_to(alive, (128, 128)).T * 2.0**-8
    lane = lax.broadcasted_iota(jnp.int32, (128, 128), 1)

    def some(q, _):
        hi, lo = split_bf16(pw[pl.ds(8 * q, 8)].reshape(1024, 128))
        bp = jnp.dot(jnp.concatenate([hi, lo], 1), e_band[...], preferred_element_type=F32)
        bp = bp.reshape(8, 128, 128)
        for k in range(8):
            gain = lax.rsqrt(bp[k] * (1.0 / BAND) + 1e-6) * alive
            if k == 0:
                gain = jnp.where((lane == 0) & (q == 0), gain * math.sqrt(0.5), gain)
            pw[8 * q + k] = gain
        return 0

    lax.fori_loop(0, 2, some, 0)


def ifft_steps(z, twid, spec, pw):
    def inv(g, _):
        rows = pl.ds(pl.multiple_of(g * 8, 8), 8)
        for f0 in range(4):
            vals = []
            for f1 in range(4):
                f = 4 * f1 + f0
                k = pw[f, rows]
                vals.append((spec[0, f, rows] * k, spec[1, f, rows] * k))
            even = cfft(vals, 1)
            odd = cfft([crot(vals[i], i, 8, 1) for i in range(4)], 1)
            for s0 in range(8):
                a = (even if s0 % 2 == 0 else odd)[s0 // 2]
                a = crot(a, f0 * s0, 32, 1)
                z[0, 8 * f0 + s0, rows], z[1, 8 * f0 + s0, rows] = a
        for s0 in range(8):
            vals = [(z[0, 8 * f0 + s0, rows], z[1, 8 * f0 + s0, rows]) for f0 in range(4)]
            vals = cfft(vals, 1)
            for s1 in range(4):
                s = 8 * s1 + s0
                a = vals[s1]
                if s:
                    c, n = twid[0, s : s + 1], twid[1, s : s + 1]
                    a = a[0] * c - a[1] * n, a[1] * c + a[0] * n
                z[0, s, rows], z[1, s, rows] = a
        return 0

    lax.fori_loop(0, 16, inv, 0)


def idft_lanes(z, e_inv, r):
    def some(q, _):
        at = pl.ds(8 * q, 8)
        both = jnp.concatenate([z[0, at].reshape(1024, 128), z[1, at].reshape(1024, 128)], 1)
        hi, lo = split_bf16(both)
        table = e_inv[...]
        d = jnp.dot(hi, table, preferred_element_type=F32)
        d = d + jnp.dot(lo, table, preferred_element_type=F32)
        d = (d[:, :128] + d[:, 128:]).astype(BF16).reshape(8, 2, 64, 128)
        r[at, :, 0:128] = d[:, 0]
        r[at, :, 128:256] = d[:, 1]
        return 0

    lax.fori_loop(0, 4, some, 0)


def whiten_begin(x, e_fwd, xt, z):
    transpose_in(x, xt)
    dft_lanes(xt, e_fwd, z)


def whiten_end(live, e_inv, e_band, twid, r, z, spec, pw):
    fft_steps(z, twid, spec, pw)
    gains(live, e_band, pw)
    ifft_steps(z, twid, spec, pw)
    idft_lanes(z, e_inv, r)


def prepare_own(r, lhs, lhs0):
    def cols(g, _):
        rows = pl.ds(pl.multiple_of(g * 16, 16), 16)
        for h in range(2):
            lanes = slice(128 * h, 128 * h + 128)
            spectra = []
            for n0 in range(2):
                vals = [r[2 * n1 + n0, rows, lanes].astype(F32) for n1 in range(16)]
                vals += [pltpu.roll(v, 127, 1) for v in vals]
                spectra.append(rfft_bins(vals))
            b0, b1 = spectra
            for e, k in enumerate((0, 16)):
                last = b0[k][0] if k == 0 else -b0[k][0]
                for n0, v in enumerate((b0[k][0], b1[k][0], last)):
                    lhs0[e, n0, rows, lanes] = v.astype(BF16)
            for k in range(1, 16):
                for n0, v in enumerate((b0[k], b1[k], crot(b0[k], k, 32, 1))):
                    re, im = (2.0 * v[0]).astype(BF16), (2.0 * v[1]).astype(BF16)
                    lhs[k - 1, 3 * n0, rows, lanes] = re
                    lhs[k - 1, 3 * n0 + 1, rows, lanes] = im
                    lhs[k - 1, 3 * n0 + 2, rows, lanes] = -re
        return 0

    lax.fori_loop(0, 4, cols, 0)


def prepare_partner(p, rhs, rhs0):
    def cols(g, _):
        rows = pl.ds(pl.multiple_of(g * 16, 16), 16)
        for h in range(2):
            lanes = slice(128 * h, 128 * h + 128)
            for s0 in range(2):
                vals = [p[2 * s1 + s0, rows, lanes].astype(F32) for s1 in range(16)] + [None] * 16
                bins = rfft_bins(vals)
                c0 = 256 * s0 + 128 * h
                for e, k in enumerate((0, 16)):
                    rhs0[e, rows, c0 : c0 + 128] = bins[k][0].astype(BF16)
                c0 = 512 * s0 + 128 * h
                for k in range(1, 16):
                    rhs[k - 1, rows, c0 : c0 + 128] = bins[k][0].astype(BF16)
                    rhs[k - 1, rows, c0 + 256 : c0 + 384] = bins[k][1].astype(BF16)
        return 0

    lax.fori_loop(0, 4, cols, 0)


def turned(v):
    tiles = [v[:, i : i + 128] for i in range(0, v.shape[1], 128)]
    rows = []
    for b in range(4):
        rows.append(v if b == 2 else jnp.concatenate([pltpu.roll(a, (b - 2) % 128, 1) for a in tiles], 1))
    return jnp.concatenate(rows, 0)


def multiply(lhs, lhs0, rhs, rhs0, y):
    def product(quads, partner):
        a = jnp.concatenate([jnp.concatenate(q, 1) for q in quads], 0)
        return lax.dot_general(a, turned(partner), NT, preferred_element_type=F32)

    for e, k in enumerate((0, 16)):
        a = [lhs0[e, n0] for n0 in range(3)]
        y[k] = product((a[:2], a[1:]), rhs0[e]).reshape(2, 64, 256)
    for k in range(15):
        re, im, neg = ([lhs[k, 3 * n0 + c] for n0 in range(3)] for c in range(3))
        quads = [(re[n], im[n], re[n + 1], im[n + 1]) for n in range(2)]
        quads += [(im[n], neg[n], im[n + 1], neg[n + 1]) for n in range(2)]
        d = product(quads, rhs[k])
        y[k + 1] = d[:128].reshape(2, 64, 256)
        y[k + 17] = d[128:].reshape(2, 64, 256)


def to_lags(y, t, scale):
    def cols(g, _):
        rows = pl.ds(pl.multiple_of(g * 8, 8), 8)
        for k0 in range(2):
            for h in range(2):
                lanes = slice(128 * h, 128 * h + 128)
                bins = {}
                for k in range(17):
                    re = y[k, k0, rows, lanes]
                    im = y[k + 16, k0, rows, lanes] if 0 < k < 16 else None
                    bins[k] = (re, im)
                vals = irfft_real(bins, 32, keep_half=True)
                for k1 in range(16):
                    at = pl.ds(pl.multiple_of(16 * (2 * k1 + k0) + 8 * (g % 2), 8), 8)
                    t[g // 2, h, at, :] = vals[k1] * scale
        return 0

    lax.fori_loop(0, 8, cols, 0)


def place(t, out):
    low = lax.broadcasted_iota(jnp.int32, (32, 128), 1) < 64
    for q in range(4):
        for i in range(0, 16, 2):
            parts = []
            for h in range(2):
                u = t[0, q, h, pl.ds(i, 32, stride=16), :]
                v = t[0, q, h, pl.ds(i + 1, 32, stride=16), :]
                parts.append(jnp.where(low, u, pltpu.roll(v, 64, 1)))
                parts.append(jnp.where(low, pltpu.roll(u, 64, 1), v))
            m = jnp.concatenate(parts, 0).T
            out[0, 16 * q + i] = m[:64]
            out[0, 16 * q + i + 1] = m[64:]


MESH = pl.DeviceIdType.MESH


def whole(chips, x, live, reach, e_fwd, e_inv, e_band, twid, out, xt, z, spec, pw, x_far, live_far, parts, lhs, lhs0, rhs, rhs0, y, t, sent, got, done):
    fibre = lax.axis_index("fibre")
    half = lax.axis_index("freq")
    c, core = fibre // 2, fibre % 2
    column = c % 4
    near = half == 0
    far = half == 1
    on_a = core == 0
    on_b = core == 1
    own = 4 * half

    def has(k):
        return c + k < chips

    def back(k):
        return c - k >= 0

    barrier = pltpu.get_barrier_semaphore()
    greeted = jnp.int32(0)

    def greet(when, chip, its_core, its_half):
        @pl.when(when)
        def _():
            pl.semaphore_signal(
                barrier, inc=1, device_id=(2 * chip + its_core, its_half), device_id_type=MESH
            )

        return jnp.where(when, 1, 0)

    for k in range(-4, 5):
        within = (c + k >= 0) & (c + k < chips)
        if k:
            greeted = greeted + greet(within, c + k, core, half)
        greeted = greeted + greet(within, c + k, 1 - core, half)
    greeted = greeted + greet(near & on_b & back(3), c - 3, 0, 1)
    greeted = greeted + greet(far & on_a & has(3), c + 3, 1, 0)

    whiten_begin(x, e_fwd, xt, z)
    pl.semaphore_wait(barrier, greeted)

    def copy(n, src, dst, chip, its_core, its_half):
        return pltpu.make_async_remote_copy(
            src_ref=parts.at[src] if isinstance(src, (int, jax.Array)) else src,
            dst_ref=parts.at[dst] if isinstance(dst, (int, jax.Array)) else dst,
            send_sem=sent.at[n],
            recv_sem=got.at[n],
            device_id=(2 * chip + its_core, its_half),
            device_id_type=MESH,
        )

    own_a1 = far & on_a & (column == 3) & back(3)
    own_a2 = far & on_a & (column >= 2) & back(2)
    relay_a3 = far & on_b & (column <= 2) & has(4)
    relay_a2 = far & on_b & (column <= 1) & has(4)
    flows = {
        "A1": (near & on_a & back(1), copy(0, 0, 1, c - 1, 1, 0), near & on_b & has(1)),
        "B1": (near & on_b & back(1), copy(1, 0, 2, c - 1, 1, 0), near & on_b & has(1)),
        "A2": (near & on_a & back(2), copy(2, 0, 3, c - 2, 1, 0), near & on_b & has(2)),
        "B0": (near & on_b, copy(3, 0, 1, c, 0, 0), near & on_a),
        "A1s": (near & on_b & has(1), copy(4, 1, 2, c, 0, 0), near & on_a & has(1)),
        "B1s": (near & on_b & has(1), copy(5, 2, 3, c, 0, 0), near & on_a & has(1)),
        "fX4": (far & on_a & back(4), copy(6, x, x_far, c - 4, 1, 1), far & on_b & has(4)),
        "fL4": (far & on_a & back(4), copy(14, live, live_far, c - 4, 1, 1), far & on_b & has(4)),
        "fA3own": (own_a1, copy(7, 4, 1, c - 3, 1, 1), far & on_b & has(3)),
        "fA3": (relay_a3, copy(7, 3, 1, c + 1, 1, 1), None),
        "fA2own": (own_a2, copy(8, 4, 0, c - 2, 0, 1), far & on_a & has(2)),
        "fA2": (relay_a2, copy(8, 3, 0, c + 2, 0, 1), None),
        "fB2": (far & on_b & back(2), copy(9, 4, 1, c - 2, 0, 1), far & on_a & has(2)),
        "fB3": (near & on_b & back(3), copy(10, 0, 3, c - 3, 0, 1), far & on_a & has(3)),
        "fA3s": (far & on_b & has(3), copy(11, 1, 2, c, 0, 1), far & on_a & has(3)),
        "fB2s": (far & on_a & has(2), copy(12, 1, 0, c, 1, 1), far & on_b & has(2)),
        "fB3s": (far & on_a & has(3), copy(13, 3, 2, c, 1, 1), far & on_b & has(3)),
    }

    def send(name):
        @pl.when(flows[name][0])
        def _():
            flows[name][1].start()

    def receive(name):
        @pl.when(flows[name][2])
        def _():
            flows[name][1].wait_recv()

    send("fX4"), send("fL4")
    whiten_end(live, e_inv, e_band, twid, parts.at[own], z, spec, pw)
    for name in ("fA3own", "fA2own", "A1", "B0"):
        send(name)

    receive("fX4"), receive("fL4")
    send("fB2")

    @pl.when(far & on_b & has(4))
    def _():
        whiten_begin(x_far, e_fwd, xt, z)
        whiten_end(live_far, e_inv, e_band, twid, parts.at[3], z, spec, pw)

    send("fA3"), send("fA2")
    prepare_own(parts.at[own], lhs, lhs0)

    def order(n):
        a0, b0, a1, b1 = ((0, 0, 1, 3), (1, 1, 3, 0), (2, 2, 2, 2), (3, 3, 0, 1))[n]
        return jnp.where(near, jnp.where(on_a, a0, b0), jnp.where(on_a, a1, b1))

    def store(n):
        return pltpu.make_async_copy(t.at[n % 2], out.at[order(n)], done.at[n % 2])

    for n in range(OFF // 2):
        if n == 0:
            receive("fB2"), send("fB2s")
        elif n == 1:
            send("B1"), send("A2")
            receive("B0")
            receive("A1"), send("A1s")
            receive("fB3"), send("fB3s")
            receive("fB2s")
        elif n == 2:
            send("fB3")
            receive("B1"), send("B1s")
            receive("A1s")
            receive("fA3own"), send("fA3s")
            receive("fA3s")
            receive("fB3s")
        else:
            receive("B1s")
            receive("A2")
            receive("fA2own")
        m = order(n)
        step = half * (OFF // 2) + m

        @pl.when(fibre + step >= 2 * chips)
        def _():
            parts[m] = jnp.zeros(parts.shape[1:], parts.dtype)

        prepare_partner(parts.at[m], rhs, rhs0)
        multiply(lhs, lhs0, rhs, rhs0, y)
        keep = jnp.where(step < reach[0], 0.5 / 32, 0.0).astype(F32)
        if n >= 2:
            store(n - 2).wait()
        to_lags(y, t.at[n % 2], keep)
        store(n).start()
    store(2).wait()
    store(3).wait()
    for name in flows:

        @pl.when(flows[name][0])
        def _():
            flows[name][1].wait_send()


def per_device(chips, traces, live, reach):
    vmem = pl.BlockSpec(memory_space=pltpu.VMEM)
    tables = [jnp.asarray(a) for a in make_tables()]
    lags = pl.pallas_call(
        functools.partial(whole, chips),
        out_shape=jax.ShapeDtypeStruct((OFF // 2, 4, 2, 512, 128), F32),
        in_specs=[vmem, vmem, pl.BlockSpec(memory_space=pltpu.SMEM)] + [vmem] * 4,
        out_specs=pl.BlockSpec(memory_space=pl.ANY),
        scratch_shapes=[
            pltpu.VMEM((4096, 128), F32),
            pltpu.VMEM((2, 32, 128, 128), F32),
            pltpu.VMEM((2, 16, 128, 128), F32),
            pltpu.VMEM((16, 128, 128), F32),
            pltpu.VMEM((2, 64, 4096), BF16),
            pltpu.VMEM((1, 64), jnp.int32),
            pltpu.VMEM((5, 32, 64, 256), BF16),
            pltpu.VMEM((15, 9, 64, 256), BF16),
            pltpu.VMEM((2, 3, 64, 256), BF16),
            pltpu.VMEM((15, 64, 1024), BF16),
            pltpu.VMEM((2, 64, 512), BF16),
            pltpu.VMEM((32, 2, 64, 256), F32),
            pltpu.VMEM((2, 4, 2, 512, 128), F32),
            pltpu.SemaphoreType.DMA((15,)),
            pltpu.SemaphoreType.DMA((15,)),
            pltpu.SemaphoreType.DMA((2,)),
        ],
        compiler_params=pltpu.CompilerParams(
            vmem_limit_bytes=60 * 2**20, collective_id=0, has_side_effects=True
        ),
    )(traces, live.reshape(1, 64), reach, *tables)
    out = pl.pallas_call(
        place,
        out_shape=jax.ShapeDtypeStruct((OFF // 2, 64, 64, LAGS), F32),
        grid=(OFF // 2,),
        in_specs=[pl.BlockSpec((1, 4, 2, 512, 128), lambda m: (m, 0, 0, 0, 0))],
        out_specs=pl.BlockSpec((1, 64, 64, LAGS), lambda m: (m, 0, 0, 0)),
    )(lags)
    return out[None]


def solution(mesh):
    placed = (P(None, "fibre", None), P("fibre"), P("fibre"))
    return jax.shard_map(
        functools.partial(per_device, mesh.shape["fibre"] // 2),
        mesh=mesh,
        in_specs=placed,
        out_specs=P("fibre", "freq", None, None, None),
        check_vma=False,
    )
```

```python
import functools
import math

import jax
import jax.numpy as jnp
import numpy as np
from jax import lax
from jax.experimental import pallas as pl
from jax.experimental.pallas import tpu as pltpu
from jax.sharding import PartitionSpec as P

BAND = 64
OFF = 8
LAGS = 128
F32 = jnp.float32
BF16 = jnp.bfloat16
NT = (((1,), (1,)), ((), ()))


def split_bf16(a):
    hi = a.astype(BF16)
    return hi, (a - hi.astype(F32)).astype(BF16)


def np_split(a):
    import ml_dtypes

    hi = a.astype(np.float32).astype(ml_dtypes.bfloat16)
    lo = (a - hi.astype(np.float64)).astype(np.float32).astype(ml_dtypes.bfloat16)
    return hi, lo


def make_tables():
    l = np.arange(128)
    ang = 2 * np.pi * (np.outer(l, l) % 128) / 128
    fwd = np.concatenate([np.cos(ang), -np.sin(ang)], 1)
    inv = np.concatenate([np.cos(ang), -np.sin(ang)], 0)
    fh, fl = np_split(fwd)
    ih, il = np_split(inv)
    e_fwd = np.concatenate([fh, fl], 0)
    e_inv = np.concatenate([ih, il], 1)
    band = (l[:, None] // BAND == l[None, :] // BAND).astype(np.float32)
    e_band = np.concatenate([band, band], 0).astype(fh.dtype)
    tw = 2 * np.pi * np.outer(np.arange(32), l) / 4096
    twid = np.stack([np.cos(tw), np.sin(tw)]).astype(np.float32)
    return e_fwd, e_inv, e_band, twid


def cadd(a, b):
    return a[0] + b[0], a[1] + b[1]


def csub(a, b):
    return a[0] - b[0], a[1] - b[1]


def cmul_i(a, sign):
    return (-a[1], a[0]) if sign > 0 else (a[1], -a[0])


def crot(a, num, den, sign):
    num %= den
    if num == 0:
        return a
    if 4 * num == den:
        return cmul_i(a, sign)
    if 2 * num == den:
        return -a[0], -a[1]
    if 4 * num == 3 * den:
        return cmul_i(a, -sign)
    if 8 * num % den == 0:
        h = math.sqrt(0.5)
        c = math.copysign(h, math.cos(2 * math.pi * num / den))
        s = sign * math.copysign(h, math.sin(2 * math.pi * num / den))
        if c > 0 and s > 0:
            return (a[0] - a[1]) * h, (a[0] + a[1]) * h
        if c > 0:
            return (a[0] + a[1]) * h, (a[1] - a[0]) * h
        if s > 0:
            return (a[0] + a[1]) * -h, (a[0] - a[1]) * h
        return (a[1] - a[0]) * h, (a[0] + a[1]) * -h
    c = math.cos(2 * math.pi * num / den)
    s = sign * math.sin(2 * math.pi * num / den)
    return a[0] * c - a[1] * s, a[0] * s + a[1] * c


def cfft(xs, sign):
    n = len(xs)
    if n == 1:
        return xs
    half = n // 2
    even = cfft([cadd(xs[i], xs[i + half]) for i in range(half)], sign)
    odd = cfft([crot(csub(xs[i], xs[i + half]), i, n, sign) for i in range(half)], sign)
    out = [None] * n
    out[0::2] = even
    out[1::2] = odd
    return out


def rfft_bins(xs):
    n = len(xs)
    if n == 1:
        return {0: (xs[0], None)}
    half = n // 2
    if xs[half] is None:
        e = d = xs[:half]
    else:
        e = [xs[i] + xs[i + half] for i in range(half)]
        d = [xs[i] - xs[i + half] for i in range(half)]
    out = {2 * k: v for k, v in rfft_bins(e).items()}
    if n == 2:
        out[1] = (d[0], None)
        return out
    q = n // 4
    z = [crot((d[s], -d[s + q]), s, n, -1) for s in range(q)]
    z = cfft(z, -1)
    for v in range(q):
        k = 4 * v + 1
        if k <= half:
            out[k] = z[v]
        else:
            out[n - k] = (z[v][0], -z[v][1])
    return out


def irfft_real(bins, n, keep_half=False):
    if n == 1:
        return [bins[0][0]]
    half = n // 2
    e = irfft_real({k // 2: v for k, v in bins.items() if k % 2 == 0}, half)
    if n == 2:
        d = [bins[1][0]]
    else:
        q = n // 4
        z = []
        for v in range(q):
            k = 4 * v + 1
            if k <= half:
                z.append(bins[k])
            else:
                re, im = bins[n - k]
                z.append((re, -im))
        z = cfft(z, 1)
        y = [crot(z[s], s, n, 1) for s in range(q)]
        d = [v[0] for v in y] + [-v[1] for v in y]
    lower = [e[i] + d[i] for i in range(half)]
    if keep_half:
        return lower
    return lower + [e[i] - d[i] for i in range(half)]


def transpose_in(x, xt):
    def tr(q, _):
        col = pl.ds(pl.multiple_of(q * 128, 128), 128)
        part = jnp.concatenate([x[0, :, col], x[1, :, col]], 0)
        xt[col] = part.T.astype(F32)
        return 0

    lax.fori_loop(0, 32, tr, 0, unroll=8)


def dft_lanes(xt, e_fwd, z):
    def some(q, _):
        v = [xt[pl.ds(8 * q + k, 128, stride=32), :].T.astype(BF16) for k in range(8)]
        v = jnp.concatenate(v, 0)
        g = jnp.dot(jnp.concatenate([v, v], 1), e_fwd[...], preferred_element_type=F32)
        g = g.reshape(8, 128, 256)
        z[0, pl.ds(8 * q, 8)] = g[:, :, :128]
        z[1, pl.ds(8 * q, 8)] = g[:, :, 128:]
        return 0

    lax.fori_loop(0, 4, some, 0)


def fft_steps(z, twid, spec, pw):
    def fwd(g, _):
        rows = pl.ds(pl.multiple_of(g * 8, 8), 8)
        for s0 in range(8):
            vals = []
            for s1 in range(4):
                s = 8 * s1 + s0
                a = z[0, s, rows], z[1, s, rows]
                if s:
                    c, n = twid[0, s : s + 1], twid[1, s : s + 1]
                    a = a[0] * c + a[1] * n, a[1] * c - a[0] * n
                vals.append(a)
            vals = cfft(vals, -1)
            for f0 in range(4):
                a = crot(vals[f0], f0 * s0, 32, -1)
                z[0, 8 * f0 + s0, rows], z[1, 8 * f0 + s0, rows] = a
        for f0 in range(4):
            vals = [(z[0, 8 * f0 + s0, rows], z[1, 8 * f0 + s0, rows]) for s0 in range(8)]
            vals = cfft(vals, -1)
            for f1 in range(4):
                f = 4 * f1 + f0
                spec[0, f, rows], spec[1, f, rows] = vals[f1]
                pw[f, rows] = vals[f1][0] * vals[f1][0] + vals[f1][1] * vals[f1][1]
        return 0

    lax.fori_loop(0, 16, fwd, 0)


def gains(live, e_band, pw):
    alive = jnp.concatenate([live[...], live[...]], 1).astype(F32)
    alive = jnp.broadcast_to(alive, (128, 128)).T * 2.0**-8
    lane = lax.broadcasted_iota(jnp.int32, (128, 128), 1)

    def some(q, _):
        hi, lo = split_bf16(pw[pl.ds(8 * q, 8)].reshape(1024, 128))
        bp = jnp.dot(jnp.concatenate([hi, lo], 1), e_band[...], preferred_element_type=F32)
        bp = bp.reshape(8, 128, 128)
        for k in range(8):
            gain = lax.rsqrt(bp[k] * (1.0 / BAND) + 1e-6) * alive
            if k == 0:
                gain = jnp.where((lane == 0) & (q == 0), gain * math.sqrt(0.5), gain)
            pw[8 * q + k] = gain
        return 0

    lax.fori_loop(0, 2, some, 0)


def ifft_steps(z, twid, spec, pw):
    def inv(g, _):
        rows = pl.ds(pl.multiple_of(g * 8, 8), 8)
        for f0 in range(4):
            vals = []
            for f1 in range(4):
                f = 4 * f1 + f0
                k = pw[f, rows]
                vals.append((spec[0, f, rows] * k, spec[1, f, rows] * k))
            even = cfft(vals, 1)
            odd = cfft([crot(vals[i], i, 8, 1) for i in range(4)], 1)
            for s0 in range(8):
                a = (even if s0 % 2 == 0 else odd)[s0 // 2]
                a = crot(a, f0 * s0, 32, 1)
                z[0, 8 * f0 + s0, rows], z[1, 8 * f0 + s0, rows] = a
        for s0 in range(8):
            vals = [(z[0, 8 * f0 + s0, rows], z[1, 8 * f0 + s0, rows]) for f0 in range(4)]
            vals = cfft(vals, 1)
            for s1 in range(4):
                s = 8 * s1 + s0
                a = vals[s1]
                if s:
                    c, n = twid[0, s : s + 1], twid[1, s : s + 1]
                    a = a[0] * c - a[1] * n, a[1] * c + a[0] * n
                z[0, s, rows], z[1, s, rows] = a
        return 0

    lax.fori_loop(0, 16, inv, 0)


def idft_lanes(z, e_inv, r):
    def some(q, _):
        at = pl.ds(8 * q, 8)
        both = jnp.concatenate([z[0, at].reshape(1024, 128), z[1, at].reshape(1024, 128)], 1)
        hi, lo = split_bf16(both)
        table = e_inv[...]
        d = jnp.dot(hi, table, preferred_element_type=F32)
        d = d + jnp.dot(lo, table, preferred_element_type=F32)
        d = (d[:, :128] + d[:, 128:]).astype(BF16).reshape(8, 2, 64, 128)
        r[at, :, 0:128] = d[:, 0]
        r[at, :, 128:256] = d[:, 1]
        return 0

    lax.fori_loop(0, 4, some, 0)


def whiten_begin(x, e_fwd, xt, z):
    transpose_in(x, xt)
    dft_lanes(xt, e_fwd, z)


def whiten_end(live, e_inv, e_band, twid, r, z, spec, pw):
    fft_steps(z, twid, spec, pw)
    gains(live, e_band, pw)
    ifft_steps(z, twid, spec, pw)
    idft_lanes(z, e_inv, r)


def prepare_own(r, lhs, lhs0):
    def cols(g, _):
        rows = pl.ds(pl.multiple_of(g * 16, 16), 16)
        for h in range(2):
            lanes = slice(128 * h, 128 * h + 128)
            spectra = []
            for n0 in range(2):
                vals = [r[2 * n1 + n0, rows, lanes].astype(F32) for n1 in range(16)]
                vals += [pltpu.roll(v, 127, 1) for v in vals]
                spectra.append(rfft_bins(vals))
            b0, b1 = spectra
            for e, k in enumerate((0, 16)):
                last = b0[k][0] if k == 0 else -b0[k][0]
                for n0, v in enumerate((b0[k][0], b1[k][0], last)):
                    lhs0[e, n0, rows, lanes] = v.astype(BF16)
            for k in range(1, 16):
                for n0, v in enumerate((b0[k], b1[k], crot(b0[k], k, 32, 1))):
                    re, im = (2.0 * v[0]).astype(BF16), (2.0 * v[1]).astype(BF16)
                    lhs[k - 1, 3 * n0, rows, lanes] = re
                    lhs[k - 1, 3 * n0 + 1, rows, lanes] = im
                    lhs[k - 1, 3 * n0 + 2, rows, lanes] = -re
        return 0

    lax.fori_loop(0, 4, cols, 0)


def prepare_partner(p, rhs, rhs0):
    def cols(g, _):
        rows = pl.ds(pl.multiple_of(g * 16, 16), 16)
        for h in range(2):
            lanes = slice(128 * h, 128 * h + 128)
            for s0 in range(2):
                vals = [p[2 * s1 + s0, rows, lanes].astype(F32) for s1 in range(16)] + [None] * 16
                bins = rfft_bins(vals)
                c0 = 256 * s0 + 128 * h
                for e, k in enumerate((0, 16)):
                    rhs0[e, rows, c0 : c0 + 128] = bins[k][0].astype(BF16)
                c0 = 512 * s0 + 128 * h
                for k in range(1, 16):
                    rhs[k - 1, rows, c0 : c0 + 128] = bins[k][0].astype(BF16)
                    rhs[k - 1, rows, c0 + 256 : c0 + 384] = bins[k][1].astype(BF16)
        return 0

    lax.fori_loop(0, 4, cols, 0)


def turned(v):
    tiles = [v[:, i : i + 128] for i in range(0, v.shape[1], 128)]
    rows = []
    for b in range(4):
        rows.append(v if b == 2 else jnp.concatenate([pltpu.roll(a, (b - 2) % 128, 1) for a in tiles], 1))
    return jnp.concatenate(rows, 0)


def multiply(lhs, lhs0, rhs, rhs0, y):
    def product(quads, partner):
        a = jnp.concatenate([jnp.concatenate(q, 1) for q in quads], 0)
        return lax.dot_general(a, turned(partner), NT, preferred_element_type=F32)

    for e, k in enumerate((0, 16)):
        a = [lhs0[e, n0] for n0 in range(3)]
        y[k] = product((a[:2], a[1:]), rhs0[e]).reshape(2, 64, 256)
    for k in range(15):
        re, im, neg = ([lhs[k, 3 * n0 + c] for n0 in range(3)] for c in range(3))
        quads = [(re[n], im[n], re[n + 1], im[n + 1]) for n in range(2)]
        quads += [(im[n], neg[n], im[n + 1], neg[n + 1]) for n in range(2)]
        d = product(quads, rhs[k])
        y[k + 1] = d[:128].reshape(2, 64, 256)
        y[k + 17] = d[128:].reshape(2, 64, 256)


def to_lags(y, t, scale):
    def cols(g, _):
        rows = pl.ds(pl.multiple_of(g * 8, 8), 8)
        for k0 in range(2):
            for h in range(2):
                lanes = slice(128 * h, 128 * h + 128)
                bins = {}
                for k in range(17):
                    re = y[k, k0, rows, lanes]
                    im = y[k + 16, k0, rows, lanes] if 0 < k < 16 else None
                    bins[k] = (re, im)
                vals = irfft_real(bins, 32, keep_half=True)
                for k1 in range(16):
                    at = pl.ds(pl.multiple_of(16 * (2 * k1 + k0) + 8 * (g % 2), 8), 8)
                    t[g // 2, h, at, :] = vals[k1] * scale
        return 0

    lax.fori_loop(0, 8, cols, 0)


def place(t, out):
    low = lax.broadcasted_iota(jnp.int32, (32, 128), 1) < 64
    for q in range(4):
        for i in range(0, 16, 2):
            parts = []
            for h in range(2):
                u = t[0, q, h, pl.ds(i, 32, stride=16), :]
                v = t[0, q, h, pl.ds(i + 1, 32, stride=16), :]
                parts.append(jnp.where(low, u, pltpu.roll(v, 64, 1)))
                parts.append(jnp.where(low, pltpu.roll(u, 64, 1), v))
            m = jnp.concatenate(parts, 0).T
            out[0, 16 * q + i] = m[:64]
            out[0, 16 * q + i + 1] = m[64:]


MESH = pl.DeviceIdType.MESH


def whole(chips, x, live, reach, e_fwd, e_inv, e_band, twid, out, xt, z, spec, pw, x_far, live_far, parts, lhs, lhs0, rhs, rhs0, y, t, sent, got, done):
    fibre = lax.axis_index("fibre")
    half = lax.axis_index("freq")
    c, core = fibre // 2, fibre % 2
    column = c % 4
    near = half == 0
    far = half == 1
    on_a = core == 0
    on_b = core == 1
    own = 4 * half

    def has(k):
        return c + k < chips

    def back(k):
        return c - k >= 0

    barrier = pltpu.get_barrier_semaphore()
    greeted = jnp.int32(0)

    def greet(when, chip, its_core, its_half):
        @pl.when(when)
        def _():
            pl.semaphore_signal(
                barrier, inc=1, device_id=(2 * chip + its_core, its_half), device_id_type=MESH
            )

        return jnp.where(when, 1, 0)

    for k in range(-4, 5):
        within = (c + k >= 0) & (c + k < chips)
        if k:
            greeted = greeted + greet(within, c + k, core, half)
        greeted = greeted + greet(within, c + k, 1 - core, half)
    greeted = greeted + greet(near & on_b & back(3), c - 3, 0, 1)
    greeted = greeted + greet(far & on_a & has(3), c + 3, 1, 0)

    whiten_begin(x, e_fwd, xt, z)
    pl.semaphore_wait(barrier, greeted)

    def copy(n, src, dst, chip, its_core, its_half):
        return pltpu.make_async_remote_copy(
            src_ref=parts.at[src] if isinstance(src, (int, jax.Array)) else src,
            dst_ref=parts.at[dst] if isinstance(dst, (int, jax.Array)) else dst,
            send_sem=sent.at[n],
            recv_sem=got.at[n],
            device_id=(2 * chip + its_core, its_half),
            device_id_type=MESH,
        )

    own_a1 = far & on_a & (column == 3) & back(3)
    own_a2 = far & on_a & (column >= 2) & back(2)
    relay_a3 = far & on_b & (column <= 2) & has(4)
    relay_a2 = far & on_b & (column <= 1) & has(4)
    flows = {
        "A1": (near & on_a & back(1), copy(0, 0, 1, c - 1, 1, 0), near & on_b & has(1)),
        "B1": (near & on_b & back(1), copy(1, 0, 2, c - 1, 1, 0), near & on_b & has(1)),
        "A2": (near & on_a & back(2), copy(2, 0, 3, c - 2, 1, 0), near & on_b & has(2)),
        "B0": (near & on_b, copy(3, 0, 1, c, 0, 0), near & on_a),
        "A1s": (near & on_b & has(1), copy(4, 1, 2, c, 0, 0), near & on_a & has(1)),
        "B1s": (near & on_b & has(1), copy(5, 2, 3, c, 0, 0), near & on_a & has(1)),
        "fX4": (far & on_a & back(4), copy(6, x, x_far, c - 4, 1, 1), far & on_b & has(4)),
        "fL4": (far & on_a & back(4), copy(14, live, live_far, c - 4, 1, 1), far & on_b & has(4)),
        "fA3own": (own_a1, copy(7, 4, 1, c - 3, 1, 1), far & on_b & has(3)),
        "fA3": (relay_a3, copy(7, 3, 1, c + 1, 1, 1), None),
        "fA2own": (own_a2, copy(8, 4, 0, c - 2, 0, 1), far & on_a & has(2)),
        "fA2": (relay_a2, copy(8, 3, 0, c + 2, 0, 1), None),
        "fB2": (far & on_b & back(2) & (column < 2), copy(9, 4, 1, c - 2, 0, 1), far & on_a & has(2)),
        "fB2row": (far & on_b & (column >= 2), copy(9, 4, 1, c - 2, 0, 1), None),
        "fB3": (near & on_b & back(3) & (column < 3), copy(10, 0, 3, c - 3, 0, 1), far & on_a & has(3)),
        "fB3row": (near & on_b & (column == 3), copy(10, 0, 3, c - 3, 0, 1), None),
        "fA3s": (far & on_b & has(3), copy(11, 1, 2, c, 0, 1), far & on_a & has(3)),
        "fB2s": (far & on_a & has(2), copy(12, 1, 0, c, 1, 1), far & on_b & has(2)),
        "fB3s": (far & on_a & has(3), copy(13, 3, 2, c, 1, 1), far & on_b & has(3)),
    }

    def send(name):
        @pl.when(flows[name][0])
        def _():
            flows[name][1].start()

    def receive(name):
        @pl.when(flows[name][2])
        def _():
            flows[name][1].wait_recv()

    send("fX4"), send("fL4")
    whiten_end(live, e_inv, e_band, twid, parts.at[own], z, spec, pw)
    for name in ("fB2row", "fA3own", "fA2own", "A1", "B0"):
        send(name)

    receive("fX4"), receive("fL4")
    send("fB2")

    @pl.when(far & on_b & has(4))
    def _():
        whiten_begin(x_far, e_fwd, xt, z)
        whiten_end(live_far, e_inv, e_band, twid, parts.at[3], z, spec, pw)

    send("fA3"), send("fA2")
    prepare_own(parts.at[own], lhs, lhs0)

    def order(n):
        a0, b0, a1, b1 = ((0, 0, 1, 3), (1, 1, 3, 0), (2, 2, 2, 2), (3, 3, 0, 1))[n]
        return jnp.where(near, jnp.where(on_a, a0, b0), jnp.where(on_a, a1, b1))

    def store(n):
        return pltpu.make_async_copy(t.at[n % 2], out.at[order(n)], done.at[n % 2])

    for n in range(OFF // 2):
        if n == 0:
            receive("fB2"), send("fB2s")
        elif n == 1:
            send("B1"), send("A2"), send("fB3row")
            receive("B0")
            receive("A1"), send("A1s")
            receive("fB3"), send("fB3s")
            receive("fB2s")
        elif n == 2:
            send("fB3")
            receive("B1"), send("B1s")
            receive("A1s")
            receive("fA3own"), send("fA3s")
            receive("fA3s")
            receive("fB3s")
        else:
            receive("B1s")
            receive("A2")
            receive("fA2own")
        m = order(n)
        step = half * (OFF // 2) + m

        @pl.when(fibre + step >= 2 * chips)
        def _():
            parts[m] = jnp.zeros(parts.shape[1:], parts.dtype)

        prepare_partner(parts.at[m], rhs, rhs0)
        multiply(lhs, lhs0, rhs, rhs0, y)
        keep = jnp.where(step < reach[0], 0.5 / 32, 0.0).astype(F32)
        if n >= 2:
            store(n - 2).wait()
        to_lags(y, t.at[n % 2], keep)
        store(n).start()
    store(2).wait()
    store(3).wait()
    for name in flows:

        @pl.when(flows[name][0])
        def _():
            flows[name][1].wait_send()


def per_device(chips, traces, live, reach):
    vmem = pl.BlockSpec(memory_space=pltpu.VMEM)
    tables = [jnp.asarray(a) for a in make_tables()]
    lags = pl.pallas_call(
        functools.partial(whole, chips),
        out_shape=jax.ShapeDtypeStruct((OFF // 2, 4, 2, 512, 128), F32),
        in_specs=[vmem, vmem, pl.BlockSpec(memory_space=pltpu.SMEM)] + [vmem] * 4,
        out_specs=pl.BlockSpec(memory_space=pl.ANY),
        scratch_shapes=[
            pltpu.VMEM((4096, 128), F32),
            pltpu.VMEM((2, 32, 128, 128), F32),
            pltpu.VMEM((2, 16, 128, 128), F32),
            pltpu.VMEM((16, 128, 128), F32),
            pltpu.VMEM((2, 64, 4096), BF16),
            pltpu.VMEM((1, 64), jnp.int32),
            pltpu.VMEM((5, 32, 64, 256), BF16),
            pltpu.VMEM((15, 9, 64, 256), BF16),
            pltpu.VMEM((2, 3, 64, 256), BF16),
            pltpu.VMEM((15, 64, 1024), BF16),
            pltpu.VMEM((2, 64, 512), BF16),
            pltpu.VMEM((32, 2, 64, 256), F32),
            pltpu.VMEM((2, 4, 2, 512, 128), F32),
            pltpu.SemaphoreType.DMA((15,)),
            pltpu.SemaphoreType.DMA((15,)),
            pltpu.SemaphoreType.DMA((2,)),
        ],
        compiler_params=pltpu.CompilerParams(
            vmem_limit_bytes=60 * 2**20, collective_id=0, has_side_effects=True
        ),
    )(traces, live.reshape(1, 64), reach, *tables)
    out = pl.pallas_call(
        place,
        out_shape=jax.ShapeDtypeStruct((OFF // 2, 64, 64, LAGS), F32),
        grid=(OFF // 2,),
        in_specs=[pl.BlockSpec((1, 4, 2, 512, 128), lambda m: (m, 0, 0, 0, 0))],
        out_specs=pl.BlockSpec((1, 64, 64, LAGS), lambda m: (m, 0, 0, 0)),
    )(lags)
    return out[None]


def solution(mesh):
    placed = (P(None, "fibre", None), P("fibre"), P("fibre"))
    return jax.shard_map(
        functools.partial(per_device, mesh.shape["fibre"] // 2),
        mesh=mesh,
        in_specs=placed,
        out_specs=P("fibre", "freq", None, None, None),
        check_vma=False,
    )
```
